256 devices in a mesh: ctx: 32 (over x, z), tp: 8 (over y, core).
Axes of the slice: x: 4, y: 4, z: 8, core: 2. Of those that a mesh axis runs over, the one named last changes fastest.
Arguments:
- x_inputs: bfloat16 [16384, 8192], P('ctx', 'tp'), may hold values from -6 to 6
- state_maps: bfloat16 [16384, 2048], P('ctx', 'tp'), may hold values from -6 to 6
- z_gate: bfloat16 [16384, 8192], P('ctx', 'tp'), may hold values from -6 to 6
- step_raw: float32 [16384, 128], P('ctx', 'tp'), may hold values from -3 to 3
- step_bias: float32 [128], P('tp'), may hold values from -0.5 to 0.5
- decay_log: float32 [128], P('tp'), may hold values from -20 to -2
- skip_gain: float32 [128], P('tp'), may hold values from 0.5 to 1.5
- x_filter: bfloat16 [4, 8192], P(None, 'tp'), may hold values from -3 to 3
- state_filter: bfloat16 [4, 2048], P(None, 'tp'), may hold values from -3 to 3
- norm_gain: float32 [8192], P('tp'), may hold values from 0.1 to 1.9
- out_weight: bfloat16 [8192, 4096], P('tp'), may hold values from -0.0625 to 0.0625
Outputs:
- mixed: bfloat16 [16384, 4096], P(('ctx', 'tp'))
The draws below stay inside these ranges and needn't reach their ends.
All inputs are finite; a program needn't handle non-finite values.
Results may differ from the reference program's by a relative error of at most 0.017.
Values may be sent and summed in bfloat16 or wider, within the bound.
No kernel may reach another device: no remote copies, remote signals or barrier semaphores. Data moves between devices by JAX's collectives and lax.ppermute only.
A program may use at most 128 MiB of HBM per device.

```python
import jax
import jax.numpy as jnp
from jax import lax

D = 4096
HEADS_DEV = 16
HEAD_DIM = 64
STATE = 128
CONV = 4
TOK_DEV = 512
BLOCK = 512
GROUPS = 8
HEADS = 128
SEQ = 16384


def draw_decay_log(key, part):
    key_one = jax.random.fold_in(jax.random.fold_in(key, 11), 0)
    lowest = -jnp.log(256.0 * SEQ)
    highest = -jnp.log(16.0)
    spread = jax.random.uniform(key_one, (HEADS,), jnp.float32)
    return lowest + spread * (highest - lowest)


def draw_step_raw(key, part):
    key_one, key_two = jax.random.split(jax.random.fold_in(key, 23), 2)
    blocks = SEQ // TOK_DEV
    noise = 0.5 * jnp.clip(jax.random.normal(key_one, (SEQ, HEADS), jnp.float32), -3.0, 3.0)
    offsets = jax.random.uniform(key_two, (blocks,), jnp.float32, minval=-0.8, maxval=0.8)
    return noise + jnp.repeat(offsets, TOK_DEV)[:, None]


def block_scale(stream_key, shape, cuts, smallest, high):
    factor_of = 1.0
    for position, parts in cuts:
        steps = jax.random.uniform(jax.random.fold_in(jax.random.fold_in(stream_key, 6), position), (parts,), jnp.float32, smallest / len(cuts), high / len(cuts))
        factor_of = factor_of * jnp.repeat(jnp.exp(steps), shape[position] // parts).reshape((-1,) + (1,) * (len(shape) - 1 - position))
    return factor_of


def bell_draw(own_key, extent, scale, reach, cuts=(), kind=jnp.bfloat16):
    array = jax.random.normal(own_key, extent, jnp.float32) * scale
    if len(cuts) > 0:
        array = block_scale(own_key, extent, cuts, -0.22, 0.18) * array
    return jnp.clip(array, min=-reach, max=reach).astype(kind)


def setup_inputs(seed: int = 0) -> dict:
    splits = jax.random.split(jax.random.key(seed), 12)
    return {
        "x_inputs": bell_draw(splits[0], (SEQ, HEADS * HEAD_DIM), 1.0, 6.0, ((0, 32), (1, 8))),
        "state_maps": bell_draw(splits[1], (SEQ, GROUPS * 2 * STATE), 1.0, 6.0, ((0, 32), (1, 8))),
        "z_gate": bell_draw(splits[2], (SEQ, HEADS * HEAD_DIM), 1.0, 6.0, ((0, 32), (1, 8))),
        "step_raw": draw_step_raw(jax.random.fold_in(splits[11], 71), 0),
        "step_bias": jnp.clip(jax.random.uniform(splits[4], (HEADS,), jnp.float32, -0.5, 0.5) * block_scale(splits[4], (HEADS,), ((0, 8),), -0.4, 0.0), -0.5, 0.5),
        "decay_log": draw_decay_log(jax.random.fold_in(splits[11], 71), 0),
        "skip_gain": jnp.clip(0.5 + 1.0 * jax.random.uniform(splits[6], (HEADS,), jnp.float32) ** block_scale(splits[6], (HEADS,), ((0, 8),), -0.2, 0.2), 0.5, 1.5),
        "x_filter": bell_draw(splits[7], (CONV, HEADS * HEAD_DIM), CONV ** -0.5, 3.0, ((1, 8),)),
        "state_filter": bell_draw(splits[8], (CONV, GROUPS * 2 * STATE), CONV ** -0.5, 3.0, ((1, 8),)),
        "norm_gain": jnp.clip(1.0 + 0.18 * jax.random.normal(splits[9], (HEADS * HEAD_DIM,), jnp.float32), 0.1, 1.9),
        "out_weight": bell_draw(splits[10], (HEADS * HEAD_DIM, D), (HEADS * HEAD_DIM) ** -0.5, 0.0625, ((0, 8),)),
    }


exactness = lax.Precision.HIGHEST

def causal_conv(padded, filters, length):
    total = jnp.zeros((length, padded.shape[1]), jnp.float32)
    for offset in range(filters.shape[0]):
        total = total + filters[offset].astype(jnp.float32) * padded[offset:offset + length].astype(jnp.float32)
    return total

def block_scan(values, b_rows, c_rows, log_decay, step_size, span):
    length, head_count, head_dim = values.shape
    state_size = b_rows.shape[1]
    pieces = length // span
    inputs = (values.reshape(pieces, span, head_count, head_dim), b_rows.reshape(pieces, span, state_size), c_rows.reshape(pieces, span, state_size), log_decay.reshape(pieces, span, head_count), step_size.reshape(pieces, span, head_count))
    row_ids = lax.broadcasted_iota(jnp.int32, (span, span), 0)
    col_ids = lax.broadcasted_iota(jnp.int32, (span, span), 1)
    causal = (row_ids >= col_ids)[None]

    def advance(carried, piece):
        piece_x, piece_b, piece_c, piece_rate, piece_step = piece
        x_wide = piece_x.astype(jnp.float32)
        b_wide = piece_b.astype(jnp.float32)
        c_wide = piece_c.astype(jnp.float32)
        cumulative = jnp.cumsum(piece_rate, axis=0)
        by_head = cumulative.T
        spread = by_head[:, :, None] - by_head[:, None, :]
        decay = jnp.where(causal, jnp.exp(-jnp.where(causal, spread, 0.0)), 0.0)
        scores = jnp.dot(piece_c, piece_b.T, preferred_element_type=jnp.float32)
        weights = decay * scores[None] * piece_step.T[:, None, :]
        weights = lax.optimization_barrier(weights.astype(jnp.bfloat16)).astype(jnp.float32)
        output = jnp.einsum('hts,shp->thp', weights, x_wide, precision=exactness)
        rounded = lax.optimization_barrier(carried.astype(jnp.bfloat16)).astype(jnp.float32)
        output = output + jnp.einsum('tn,hpn->thp', c_wide, rounded, precision=exactness) * jnp.exp(-cumulative)[:, :, None]
        tail = jnp.exp(-(cumulative[-1][None, :] - cumulative)) * piece_step
        weighted = lax.optimization_barrier((tail[:, :, None] * x_wide).astype(jnp.bfloat16)).astype(jnp.float32)
        fresh = jnp.exp(-cumulative[-1])[:, None, None] * carried
        fresh = fresh + jnp.einsum('shp,sn->hpn', weighted, b_wide, precision=exactness)
        return (fresh, output)
    start_state = jnp.zeros((head_count, head_dim, state_size), jnp.float32)
    final_state, outputs = lax.scan(advance, start_state, inputs)
    return (outputs.reshape(length, head_count, head_dim), final_state)

def reference(x_inputs, state_maps, z_gate, step_raw, step_bias, decay_log, skip_gain, x_filter, state_filter, norm_gain, out_weight):
    leading = CONV - 1
    x_pad = jnp.concatenate([jnp.zeros((leading, x_inputs.shape[1]), x_inputs.dtype), x_inputs], 0)
    x_conv = jax.nn.silu(causal_conv(x_pad, x_filter, SEQ)).astype(jnp.bfloat16)
    bc_pad = jnp.concatenate([jnp.zeros((leading, state_maps.shape[1]), state_maps.dtype), state_maps], 0)
    bc_conv = jax.nn.silu(causal_conv(bc_pad, state_filter, SEQ)).astype(jnp.bfloat16)
    step_size = jax.nn.softplus(step_raw + step_bias)
    log_decay = step_size * jnp.exp(decay_log)
    channels = HEADS_DEV * HEAD_DIM
    total = jnp.zeros((SEQ, D), jnp.float32)
    for group in range(GROUPS):
        heads_here = slice(group * HEADS_DEV, (group + 1) * HEADS_DEV)
        cols = slice(group * channels, (group + 1) * channels)
        values = x_conv[:, cols].reshape(SEQ, HEADS_DEV, HEAD_DIM)
        b_rows = bc_conv[:, 2 * group * STATE:(2 * group + 1) * STATE]
        c_rows = bc_conv[:, (2 * group + 1) * STATE:(2 * group + 2) * STATE]
        output, _ = block_scan(values, b_rows, c_rows, log_decay[:, heads_here], step_size[:, heads_here], BLOCK)
        output = output + skip_gain[heads_here][None, :, None] * values.astype(jnp.float32)
        gated = output.reshape(SEQ, channels) * jax.nn.silu(z_gate[:, cols].astype(jnp.float32))
        scale = lax.rsqrt(lax.optimization_barrier(jnp.mean(gated * gated, axis=-1, keepdims=True)) + 1e-05)
        normed = (gated * scale * norm_gain[cols]).astype(jnp.bfloat16)
        partial_sum = jnp.dot(normed, out_weight[cols], preferred_element_type=jnp.float32)
        total = total + lax.optimization_barrier(partial_sum.astype(jnp.bfloat16)).astype(jnp.float32)
    return total.astype(jnp.bfloat16)
```

```python
import jax
import jax.numpy as jnp
from jax import lax
from jax.sharding import PartitionSpec as P


def shifted(value, axis, steps):
    count = lax.axis_size(axis)
    leading, last = (max(0, -steps), min(count, count - steps))
    return lax.ppermute(value, axis, [(source, source + steps) for source in range(leading, last)])


def causal_conv(padded, filters, length):
    total = jnp.zeros((length, padded.shape[1]), jnp.float32)
    for offset in range(filters.shape[0]):
        total = total + filters[offset].astype(jnp.float32) * padded[
            offset : offset + length
        ].astype(jnp.float32)
    return total


def block_scan(values, b_rows, c_rows, log_decay, step_size, span):
    length, head_count, head_dim = values.shape
    state_size = b_rows.shape[1]
    pieces = length // span
    inputs = (
        values.reshape(pieces, span, head_count, head_dim),
        b_rows.reshape(pieces, span, state_size),
        c_rows.reshape(pieces, span, state_size),
        log_decay.reshape(pieces, span, head_count),
        step_size.reshape(pieces, span, head_count),
    )
    row_ids = lax.broadcasted_iota(jnp.int32, (span, span), 0)
    col_ids = lax.broadcasted_iota(jnp.int32, (span, span), 1)
    causal = (row_ids >= col_ids)[None]

    def advance(carried, piece):
        piece_x, piece_b, piece_c, piece_rate, piece_step = piece
        cumulative = jnp.cumsum(piece_rate, axis=0)
        by_head = cumulative.T
        spread = by_head[:, :, None] - by_head[:, None, :]
        decay = jnp.where(causal, jnp.exp(-jnp.where(causal, spread, 0.0)), 0.0)
        scores = jnp.dot(piece_c, piece_b.T, preferred_element_type=jnp.float32)
        weights = (decay * scores[None] * piece_step.T[:, None, :]).astype(jnp.bfloat16)
        output = jnp.einsum("hts,shp->thp", weights, piece_x, preferred_element_type=jnp.float32)
        rounded = carried.astype(jnp.bfloat16)
        output = (
            output
            + jnp.einsum("tn,hpn->thp", piece_c, rounded, preferred_element_type=jnp.float32)
            * jnp.exp(-cumulative)[:, :, None]
        )
        tail = jnp.exp(-(cumulative[-1][None, :] - cumulative)) * piece_step
        weighted = (tail[:, :, None] * piece_x.astype(jnp.float32)).astype(jnp.bfloat16)
        fresh = jnp.exp(-cumulative[-1])[:, None, None] * carried
        fresh = fresh + jnp.einsum(
            "shp,sn->hpn", weighted, piece_b, preferred_element_type=jnp.float32
        )
        return (fresh, output)

    start_state = jnp.zeros((head_count, head_dim, state_size), jnp.float32)
    final_state, outputs = lax.scan(advance, start_state, inputs)
    return (outputs.reshape(length, head_count, head_dim), final_state)


def on_device(
    x_inputs,
    state_maps,
    z_gate,
    step_raw,
    step_bias,
    decay_log,
    skip_gain,
    x_filter,
    state_filter,
    norm_gain,
    out_weight,
):
    length = x_inputs.shape[0]
    leading = x_filter.shape[0] - 1
    channels = x_inputs.shape[1]
    head_count = step_raw.shape[1]
    head_dim = channels // head_count
    state_size = state_maps.shape[1] // 2
    prev_x, prev_maps = shifted(
        (x_inputs[length - leading :], state_maps[length - leading :]), "ctx", 1
    )
    x_conv = jax.nn.silu(
        causal_conv(jnp.concatenate([prev_x, x_inputs], 0), x_filter, length)
    ).astype(jnp.bfloat16)
    bc_conv = jax.nn.silu(
        causal_conv(jnp.concatenate([prev_maps, state_maps], 0), state_filter, length)
    ).astype(jnp.bfloat16)
    step_size = jax.nn.softplus(step_raw + step_bias)
    log_decay = step_size * jnp.exp(decay_log)
    values = x_conv.reshape(length, head_count, head_dim)
    b_rows = bc_conv[:, :state_size]
    c_rows = bc_conv[:, state_size:]
    local_out, local_state = block_scan(
        values, b_rows, c_rows, log_decay, step_size, min(length, 512)
    )
    block_count = lax.axis_size("ctx")
    block_total = jnp.sum(log_decay, axis=0)
    totals = lax.all_gather(block_total, "ctx", axis=0)
    slices = local_state.reshape(block_count, -1, state_size).astype(jnp.bfloat16)
    slices = lax.all_to_all(slices, "ctx", 0, 0, tiled=True).astype(jnp.float32)
    own = lax.axis_index("ctx") * head_count // block_count
    decays = jnp.exp(-lax.dynamic_slice_in_dim(totals, own, 1, axis=1))[:, 0]
    running = jnp.zeros_like(slices[0])
    entering = []
    for block in range(block_count):
        entering.append(running.astype(jnp.bfloat16))
        running = decays[block] * running + slices[block]
    carried = lax.all_to_all(jnp.stack(entering), "ctx", 0, 0, tiled=True)
    carried = carried.reshape(head_count, head_dim, state_size)

    cumulative = jnp.cumsum(log_decay, axis=0)
    rounded = carried
    output = (
        local_out
        + jnp.einsum("tn,hpn->thp", c_rows, rounded, preferred_element_type=jnp.float32)
        * jnp.exp(-cumulative)[:, :, None]
    )
    output = output + skip_gain[None, :, None] * values.astype(jnp.float32)
    gated = output.reshape(length, channels) * jax.nn.silu(z_gate.astype(jnp.float32))
    scale = lax.rsqrt(jnp.mean(gated * gated, axis=-1, keepdims=True) + 1e-05)
    normed = (gated * scale * norm_gain).astype(jnp.bfloat16)
    return lax.psum_scatter(
        jnp.dot(normed, out_weight, preferred_element_type=jnp.float32).astype(jnp.bfloat16),
        "tp",
        scatter_dimension=0,
        tiled=True,
    )


def solution(mesh):
    return jax.shard_map(
        on_device,
        mesh=mesh,
        in_specs=(
            P("ctx", "tp"),
            P("ctx", "tp"),
            P("ctx", "tp"),
            P("ctx", "tp"),
            P("tp"),
            P("tp"),
            P("tp"),
            P(None, "tp"),
            P(None, "tp"),
            P("tp"),
            P("tp", None),
        ),
        out_specs=P(("ctx", "tp"), None),
        check_vma=False,
    )
```

```python
import functools

import jax
import jax.numpy as jnp
from jax import lax
from jax.experimental import pallas as pl
from jax.experimental.pallas import tpu as pltpu
from jax.sharding import PartitionSpec as P

BF16 = jnp.bfloat16
F32 = jnp.float32
VMEM_LIMIT = 40 * 1024 * 1024


def params(**more):
    return pltpu.CompilerParams(vmem_limit_bytes=VMEM_LIMIT, **more)


def shifted(value, axis, steps):
    count = lax.axis_size(axis)
    leading, last = (max(0, -steps), min(count, count - steps))
    return lax.ppermute(value, axis, [(source, source + steps) for source in range(leading, last)])


def three_parts(value):
    high = value.astype(BF16)
    rest = value - high.astype(F32)
    middle = rest.astype(BF16)
    low = (rest - middle.astype(F32)).astype(BF16)
    return high, middle, low


def packed_parts(value):
    high, middle, low = three_parts(value)
    wide = [high.astype(F32), middle.astype(F32), low.astype(F32)]
    return jnp.concatenate(wide, axis=1).astype(BF16)


def head_selector(first_head, heads, head_dim, width):
    rows = lax.broadcasted_iota(jnp.int32, (3 * heads, width), 0)
    lanes = lax.broadcasted_iota(jnp.int32, (3 * heads, width), 1)
    return (rows % heads == first_head + lanes // head_dim).astype(F32).astype(BF16)


def silu(value):
    return value / (1.0 + jnp.exp(-value))


def conv_rows(padded, taps, start, rows):
    count = taps.shape[0]
    total = None
    for offset in range(count):
        first = 8 - (count - 1) + offset + start
        term = taps[offset : offset + 1] * padded[pl.ds(first, rows), :]
        total = term if total is None else total + term
    return total


def state_kernel(
    heads,
    head_dim,
    x_ref,
    halo_ref,
    x_taps_ref,
    maps_ref,
    maps_halo_ref,
    maps_taps_ref,
    raw_ref,
    bias_ref,
    decay_ref,
    conv_ref,
    maps_conv_ref,
    step_ref,
    total_ref,
    sent_ref,
    padded,
    tail_parts,
    end_parts,
    weighted,
):
    column = pl.program_id(0)
    length, width = x_ref.shape
    leading = halo_ref.shape[0]
    tile = 64
    state = maps_ref.shape[1] // 2

    def fill(source, halo):
        padded[pl.ds(8 - leading, leading), :] = halo[...].astype(F32)
        for start in range(0, length, tile):
            padded[pl.ds(8 + start, tile), :] = source[pl.ds(start, tile), :].astype(F32)

    @pl.when(column == 0)
    def _():
        step = jnp.log1p(jnp.exp(raw_ref[...] + bias_ref[...]))
        step_ref[...] = step
        rate = step * jnp.exp(decay_ref[...])
        piece = 128
        upper = lax.broadcasted_iota(jnp.int32, (piece, piece), 0)
        lower = lax.broadcasted_iota(jnp.int32, (piece, piece), 1)
        triangle = (upper >= lower).astype(F32).astype(BF16)
        before = jnp.zeros((1, heads), F32)
        for start in range(0, length, piece):
            parts = three_parts(rate[start : start + piece])
            sums = [jnp.dot(triangle, part, preferred_element_type=F32) for part in parts]
            block = sums[0] + (sums[1] + sums[2]) + before
            total_ref[pl.ds(start, piece), :] = block
            before = block[piece - 1 : piece]
        end = before
        tail_parts[...] = packed_parts(jnp.exp(total_ref[...] - end) * step)
        end_parts[...] = packed_parts(jnp.broadcast_to(jnp.exp(-end), (8, heads)))
        fill(maps_ref, maps_halo_ref)
        taps = maps_taps_ref[...].astype(F32)
        for start in range(0, length, tile):
            rows = silu(conv_rows(padded, taps, start, tile))
            maps_conv_ref[pl.ds(start, tile), :] = rows.astype(BF16)

    fill(x_ref, halo_ref)
    taps = x_taps_ref[...].astype(F32)
    selector = head_selector(column * (width // head_dim), heads, head_dim, width)
    for start in range(0, length, tile):
        rows = silu(conv_rows(padded, taps, start, tile)).astype(BF16)
        conv_ref[pl.ds(start, tile), :] = rows
        tail = jnp.dot(
            tail_parts[pl.ds(start, tile), :], selector, preferred_element_type=F32
        )
        weighted[pl.ds(start, tile), :] = (tail * rows.astype(F32)).astype(BF16)
    reached = lax.dot_general(
        maps_conv_ref[:, :state],
        weighted[...],
        (((0,), (0,)), ((), ())),
        preferred_element_type=F32,
    )
    factor = jnp.dot(end_parts[...], selector, preferred_element_type=F32)
    high, middle, low = [part.astype(F32) for part in three_parts(factor)]
    ids = lax.broadcasted_iota(jnp.int32, factor.shape, 0)
    extra = jnp.where(ids == 0, high, jnp.where(ids == 1, middle, jnp.where(ids == 2, low, 0.0)))
    per_column = sent_ref.shape[0] // (width // 128)
    depth = state // per_column
    for piece in range(sent_ref.shape[0]):
        lanes = slice(128 * (piece // per_column), 128 * (piece // per_column) + 128)
        first = depth * (piece % per_column)
        sent_ref[piece] = jnp.concatenate(
            [reached[first : first + depth, lanes], extra[:, lanes]], axis=0
        ).astype(BF16)


def local_states(x, halo, x_taps, maps, maps_taps, raw, bias, decay_log, blocks):
    length, channels = x.shape
    heads = raw.shape[1]
    maps_width = maps.shape[1]
    width = 256
    columns = channels // width
    leading = halo.shape[0]
    taps = x_taps.shape[0]
    state = maps_width // 2
    sent = (blocks, state * channels // (blocks * 128) + 8, 128)
    whole = lambda shape: pl.BlockSpec(shape, lambda i: (0,) * len(shape))
    return pl.pallas_call(
        functools.partial(state_kernel, heads, channels // heads),
        grid=(columns,),
        in_specs=[
            pl.BlockSpec((length, width), lambda i: (0, i)),
            pl.BlockSpec((leading, width), lambda i: (0, i)),
            pl.BlockSpec((taps, width), lambda i: (0, i)),
            whole((length, maps_width)),
            pl.BlockSpec((leading, maps_width), lambda i: (0, channels // maps_width)),
            whole((taps, maps_width)),
            whole((length, heads)),
            whole((1, heads)),
            whole((1, heads)),
        ],
        out_specs=[
            pl.BlockSpec((length, width), lambda i: (0, i)),
            whole((length, maps_width)),
            whole((length, heads)),
            whole((length, heads)),
            pl.BlockSpec((blocks // columns,) + sent[1:], lambda i: (i, 0, 0)),
        ],
        out_shape=[
            jax.ShapeDtypeStruct((length, channels), BF16),
            jax.ShapeDtypeStruct((length, maps_width), BF16),
            jax.ShapeDtypeStruct((length, heads), F32),
            jax.ShapeDtypeStruct((length, heads), F32),
            jax.ShapeDtypeStruct(sent, BF16),
        ],
        scratch_shapes=[
            pltpu.VMEM((length + 8, width), F32),
            pltpu.VMEM((length, 3 * heads), BF16),
            pltpu.VMEM((8, 3 * heads), BF16),
            pltpu.VMEM((length, width), BF16),
        ],
        compiler_params=params(),
        cost_estimate=pl.CostEstimate(
            flops=20_000_000_000, bytes_accessed=4_000_000, transcendentals=0
        ),
        name="local_states",
    )(x, halo, x_taps, maps, halo, maps_taps, raw, bias, decay_log)


def scan_kernel(got_ref, out_ref):
    blocks, rows, lanes = out_ref.shape
    running = jnp.zeros((rows, lanes), F32)
    for block in range(blocks):
        out_ref[block] = running.astype(BF16)
        if block < blocks - 1:
            piece = got_ref[block].astype(F32)
            factor = piece[rows : rows + 1] + (
                piece[rows + 1 : rows + 2] + piece[rows + 2 : rows + 3]
            )
            running = factor * running + piece[:rows]


def scan_blocks(got):
    blocks, rows, lanes = got.shape
    return pl.pallas_call(
        scan_kernel,
        out_shape=jax.ShapeDtypeStruct((blocks, rows - 8, lanes), BF16),
        compiler_params=params(),
        name="scan_blocks",
    )(got)


def local_kernel(
    head_dim, x_ref, maps_ref, z_ref, step_ref, total_ref, skip_ref, shown_ref, passed_ref, scores
):
    pair = pl.program_id(0)
    length, width = x_ref.shape
    state = maps_ref.shape[1] // 2
    per_step = width // head_dim
    tile = 128

    @pl.when(pair == 0)
    def _():
        scores[...] = lax.dot_general(
            maps_ref[:, state:],
            maps_ref[:, :state],
            (((1,), (1,)), ((), ())),
            preferred_element_type=F32,
        )

    later = lax.broadcasted_iota(jnp.int32, (tile, tile), 0)
    earlier = lax.broadcasted_iota(jnp.int32, (tile, tile), 1)
    causal = later >= earlier
    lanes = lax.broadcasted_iota(jnp.int32, (tile, width), 1)
    totals = total_ref[0]
    steps = step_ref[0]
    for start in range(0, length, tile):
        outs = []
        outer = None
        for head in range(per_step):
            columns = jnp.broadcast_to(totals[head : head + 1, start : start + tile], (tile, tile)).T
            weights = []
            for source in range(0, start + tile, tile):
                spread = totals[head : head + 1, source : source + tile] - columns
                if source == start:
                    spread = jnp.where(causal, spread, -1e30)
                part = jnp.exp(spread) * scores[pl.ds(start, tile), pl.ds(source, tile)]
                part = part * steps[head : head + 1, source : source + tile]
                weights.append(part.astype(BF16))
            weights = weights[0] if len(weights) == 1 else jnp.concatenate(weights, axis=1)
            outs.append(
                jnp.dot(
                    weights,
                    x_ref[pl.ds(0, start + tile), pl.ds(head * head_dim, head_dim)],
                    preferred_element_type=F32,
                )
            )
            fade = jnp.exp(-columns)
            outer = fade if outer is None else jnp.where(lanes >= head * head_dim, fade, outer)
        values = x_ref[pl.ds(start, tile), :].astype(F32)
        gate = silu(z_ref[pl.ds(start, tile), :].astype(F32))
        out = jnp.concatenate(outs, axis=1) + skip_ref[...] * values
        shown_ref[pl.ds(start, tile), :] = out * gate
        passed_ref[pl.ds(start, tile), :] = outer * gate


def local_outputs(x_conv, maps_conv, z, step_rows, total_rows, skip, head_dim):
    length, channels = x_conv.shape
    width = 128
    columns = channels // width
    heads = channels // head_dim
    per_step = heads // columns
    maps_width = maps_conv.shape[1]
    step_rows = step_rows.reshape(columns, per_step, length)
    total_rows = total_rows.reshape(columns, per_step, length)
    block = pl.BlockSpec((length, width), lambda i: (0, i))
    row_block = pl.BlockSpec((1, per_step, length), lambda i: (i, 0, 0))
    return pl.pallas_call(
        functools.partial(local_kernel, head_dim),
        grid=(columns,),
        in_specs=[
            block,
            pl.BlockSpec((length, maps_width), lambda i: (0, 0)),
            block,
            row_block,
            row_block,
            pl.BlockSpec((1, width), lambda i: (0, i)),
        ],
        out_specs=[block, block],
        out_shape=[jax.ShapeDtypeStruct((length, channels), F32)] * 2,
        scratch_shapes=[pltpu.VMEM((length, length), F32)],
        compiler_params=params(),
        cost_estimate=pl.CostEstimate(
            flops=8_000_000_000, bytes_accessed=6_000_000, transcendentals=0
        ),
        name="local_outputs",
    )(x_conv, maps_conv, z, step_rows, total_rows, skip)


def norm_kernel(picks, carried_ref, maps_ref, shown_ref, passed_ref, gain_ref, out_ref, entering):
    state, channels = entering.shape
    pieces, depth, lanes = carried_ref.shape
    per_column = state // depth

    @pl.when(pl.program_id(0) == 0)
    def _():
        for piece in range(pieces):
            entering[
                pl.ds(depth * (piece % per_column), depth),
                pl.ds(lanes * (piece // per_column), lanes),
            ] = carried_ref[piece]

    carry = jnp.dot(maps_ref[...], entering[...], preferred_element_type=F32)
    gated = shown_ref[...] + carry * passed_ref[...]
    scale = lax.rsqrt(jnp.mean(gated * gated, axis=1, keepdims=True) + 1e-05)
    out_ref[...] = (gated * scale * gain_ref[...]).astype(BF16)


def normed_rows(picks, carried, maps_conv, shown, passed, gain, name):
    length, channels = shown.shape
    state = maps_conv.shape[1] // 2
    count = picks.shape[0]
    rows = length // (2 * count)
    picked = pl.BlockSpec((rows, channels), lambda i, picks: (picks[i], 0))
    return pl.pallas_call(
        norm_kernel,
        grid_spec=pltpu.PrefetchScalarGridSpec(
            num_scalar_prefetch=1,
            grid=(count,),
            in_specs=[
                pl.BlockSpec(carried.shape, lambda i, picks: (0, 0, 0)),
                pl.BlockSpec((rows, state), lambda i, picks: (picks[i], 1)),
                picked,
                picked,
                pl.BlockSpec((1, channels), lambda i, picks: (0, 0)),
            ],
            out_specs=pl.BlockSpec((rows, channels), lambda i, picks: (i, 0)),
            scratch_shapes=[pltpu.VMEM((state, channels), BF16)],
        ),
        out_shape=jax.ShapeDtypeStruct((rows * count, channels), BF16),
        compiler_params=params(),
        cost_estimate=pl.CostEstimate(
            flops=1_000_000_000, bytes_accessed=3_000_000, transcendentals=0
        ),
        name=name,
    )(picks, carried, maps_conv, shown, passed, gain)


def project_kernel(own_ref, other_ref, own_weight_ref, other_weight_ref, *out_refs):
    product = jnp.dot(own_ref[...], own_weight_ref[...], preferred_element_type=F32)
    product = product + jnp.dot(
        other_ref[...], other_weight_ref[...], preferred_element_type=F32
    )
    rows = out_refs[0].shape[0]
    for index, out_ref in enumerate(out_refs):
        out_ref[...] = product[rows * index : rows * (index + 1)].astype(out_ref.dtype)


def project(own, other, own_weight, other_weight, part, parts, name):
    count, depth = own.shape
    columns = own_weight.shape[1] // parts
    rows = count // 4
    width = 512
    tiles = columns // width
    source = pl.BlockSpec((count, depth), lambda i: (0, 0))
    weight = pl.BlockSpec((depth, width), lambda i: (0, part * tiles + i))
    return pl.pallas_call(
        project_kernel,
        grid=(tiles,),
        in_specs=[source, source, weight, weight],
        out_specs=[pl.BlockSpec((rows, width), lambda i: (0, i))] * 4,
        out_shape=[jax.ShapeDtypeStruct((rows, columns), BF16)] * 4,
        compiler_params=params(),
        cost_estimate=pl.CostEstimate(
            flops=4 * count * depth * columns, bytes_accessed=9_000_000, transcendentals=0
        ),
        name=name,
    )(own, other, own_weight, other_weight)


def on_device(
    x_inputs,
    state_maps,
    z_gate,
    step_raw,
    step_bias,
    decay_log,
    skip_gain,
    x_filter,
    state_filter,
    norm_gain,
    out_weight,
):
    length, channels = x_inputs.shape
    leading = x_filter.shape[0] - 1
    heads = step_raw.shape[1]
    head_dim = channels // heads
    blocks = lax.axis_size("ctx")
    members = lax.axis_size("tp")
    ring = members // 2
    place = lax.axis_index("tp")
    across, core = place // 2, place % 2

    def core_swap(value):
        return lax.ppermute(value, "tp", [(i, i ^ 1) for i in range(members)])

    def along(value, steps):
        pairs = [
            (2 * y + c, 2 * ((y + steps) % ring) + c) for y in range(ring) for c in range(2)
        ]
        return lax.ppermute(value, "tp", pairs)

    ends = jnp.concatenate([x_inputs[length - leading :], state_maps[length - leading :]], axis=1)
    halo = shifted(ends, "ctx", 1)
    other_weight = core_swap(out_weight)
    x_conv, maps_conv, step, total, sent = local_states(
        x_inputs,
        halo,
        x_filter,
        state_maps,
        state_filter,
        step_raw,
        step_bias[None],
        decay_log[None],
        blocks,
    )
    got = lax.all_to_all(sent, "ctx", 0, 0, tiled=True)
    shown, passed = local_outputs(
        x_conv,
        maps_conv,
        z_gate,
        step.T,
        total.T,
        jnp.repeat(skip_gain, head_dim)[None],
        head_dim,
    )
    entering = scan_blocks(got)
    carried = lax.all_to_all(entering, "ctx", 0, 0, tiled=True)

    turns = (across + jnp.array([2, 1, 3, 0], jnp.int32)) % ring
    gain = norm_gain[None]
    give = normed_rows(2 * turns + 1 - core, carried, maps_conv, shown, passed, gain, "give_rows")
    taken = core_swap(give)
    keep = normed_rows(2 * turns + core, carried, maps_conv, shown, passed, gain, "keep_rows")
    far_a, up_a, down_a, own_a = project(keep, taken, out_weight, other_weight, 0, 2, "left_half")
    far_b, up_b, down_b, own_b = project(keep, taken, out_weight, other_weight, 1, 2, "right_half")

    def added(*values):
        return functools.reduce(lambda a, b: a + b, [v.astype(F32) for v in values]).astype(BF16)

    relay_a = along(far_a, 1)
    from_above_a = along(down_a, -1)
    relay_b = along(far_b, -1)
    from_below_b = along(up_b, 1)
    from_below_a = along(added(up_a, relay_a), 1)
    from_above_b = along(added(down_b, relay_b), -1)
    return jnp.concatenate(
        [added(own_a, from_above_a, from_below_a), added(own_b, from_above_b, from_below_b)], axis=1
    )


def solution(mesh):
    return jax.shard_map(
        on_device,
        mesh=mesh,
        in_specs=(
            P("ctx", "tp"),
            P("ctx", "tp"),
            P("ctx", "tp"),
            P("ctx", "tp"),
            P("tp"),
            P("tp"),
            P("tp"),
            P(None, "tp"),
            P(None, "tp"),
            P("tp"),
            P("tp", None),
        ),
        out_specs=P(("ctx", "tp"), None),
        check_vma=False,
    )
```

```python
import functools

import jax
import jax.numpy as jnp
from jax import lax
from jax.experimental import pallas as pl
from jax.experimental.pallas import tpu as pltpu
from jax.sharding import PartitionSpec as P

BF16 = jnp.bfloat16
F32 = jnp.float32
VMEM_LIMIT = 16 * 1024 * 1024
TURNS = (2, 1, 3, 0)


def far_memory(value):
    return pltpu.with_memory_space_constraint(value, pltpu.HBM)


def params(**more):
    return pltpu.CompilerParams(vmem_limit_bytes=VMEM_LIMIT, **more)


def shifted(value, axis, steps):
    count = lax.axis_size(axis)
    leading, last = (max(0, -steps), min(count, count - steps))
    return lax.ppermute(value, axis, [(source, source + steps) for source in range(leading, last)])


def three_parts(value):
    high = value.astype(BF16)
    rest = value - high.astype(F32)
    middle = rest.astype(BF16)
    low = (rest - middle.astype(F32)).astype(BF16)
    return high, middle, low


def packed_parts(value):
    high, middle, low = three_parts(value)
    wide = [high.astype(F32), middle.astype(F32), low.astype(F32)]
    return jnp.concatenate(wide, axis=0).astype(BF16)


def head_selector(first_head, heads, head_dim, width):
    rows = lax.broadcasted_iota(jnp.int32, (3 * heads, width), 0)
    lanes = lax.broadcasted_iota(jnp.int32, (3 * heads, width), 1)
    return (rows % heads == first_head + lanes // head_dim).astype(F32).astype(BF16)


def spread_heads(parts, selector):
    return lax.dot_general(
        parts, selector, (((0,), (0,)), ((), ())), preferred_element_type=F32
    )


def silu(value):
    return value / (1.0 + jnp.exp(-value))


def conv_rows(padded, taps, start, rows):
    count = taps.shape[0]
    total = None
    for offset in range(count):
        first = 8 - (count - 1) + offset + start
        term = taps[offset : offset + 1] * padded[pl.ds(first, rows), :]
        total = term if total is None else total + term
    return total


def state_kernel(
    heads,
    head_dim,
    held,
    x_ref,
    x_taps_ref,
    maps_ref,
    maps_taps_ref,
    raw_ref,
    bias_ref,
    decay_ref,
    conv_ref,
    maps_conv_ref,
    step_ref,
    total_ref,
    first_tail_ref,
    reached_ref,
    padded,
    tail_parts,
    end_parts,
    weighted,
):
    column = pl.program_id(0)
    length, width = x_ref.shape
    tile = 64
    state = maps_ref.shape[1] // 2

    def fill(source):
        padded[pl.ds(0, 8), :] = jnp.zeros((8, padded.shape[1]), F32)
        for start in range(0, length, tile):
            padded[pl.ds(8 + start, tile), :] = source[pl.ds(start, tile), :].astype(F32)

    @pl.when(column == 0)
    def _():
        row_ids = lax.broadcasted_iota(jnp.int32, (heads, heads), 0)
        col_ids = lax.broadcasted_iota(jnp.int32, (heads, heads), 1)

        def as_column(ref):
            spread = jnp.where(row_ids == col_ids, ref[...], 0.0)
            return jnp.sum(spread, axis=1, keepdims=True)

        step = jnp.log1p(jnp.exp(raw_ref[...] + as_column(bias_ref)))
        step_ref[...] = step
        rate = step * jnp.exp(as_column(decay_ref))
        piece = 128
        source = lax.broadcasted_iota(jnp.int32, (piece, piece), 0)
        target = lax.broadcasted_iota(jnp.int32, (piece, piece), 1)
        triangle = (source <= target).astype(F32).astype(BF16)
        before = jnp.zeros((heads, 1), F32)
        for start in range(0, length, piece):
            parts = three_parts(rate[:, start : start + piece])
            sums = [jnp.dot(part, triangle, preferred_element_type=F32) for part in parts]
            block = sums[0] + (sums[1] + sums[2]) + before
            total_ref[:, pl.ds(start, piece)] = block
            before = block[:, piece - 1 : piece]
        tail_parts[...] = packed_parts(jnp.exp(total_ref[...] - before) * step)
        end_parts[...] = packed_parts(jnp.broadcast_to(jnp.exp(-before), (heads, 128)))
        first_tail_ref[...] = tail_parts[:, :128]
        fill(maps_ref)
        taps = maps_taps_ref[...].astype(F32)
        for start in range(0, length, tile):
            rows = silu(conv_rows(padded, taps, start, tile))
            maps_conv_ref[pl.ds(start, tile), :] = rows.astype(BF16)

    fill(x_ref)
    taps = x_taps_ref[...].astype(F32)
    selector = head_selector(column * (width // head_dim), heads, head_dim, width)
    for start in range(0, length, tile):
        rows = silu(conv_rows(padded, taps, start, tile)).astype(BF16)
        conv_ref[pl.ds(start, tile), :] = rows
        tail = spread_heads(tail_parts[:, start : start + tile], selector)
        scaled = tail * rows.astype(F32)
        if start == 0:
            ids = lax.broadcasted_iota(jnp.int32, scaled.shape, 0)
            scaled = jnp.where(ids >= held, scaled, 0.0)
        weighted[pl.ds(start, tile), :] = scaled.astype(BF16)
    reached = lax.dot_general(
        maps_conv_ref[:, :state],
        weighted[...],
        (((0,), (0,)), ((), ())),
        preferred_element_type=F32,
    )
    factor = spread_heads(end_parts[:, :8], selector)
    high, middle, low = [part.astype(F32) for part in three_parts(factor)]
    ids = lax.broadcasted_iota(jnp.int32, factor.shape, 0)
    extra = jnp.where(ids == 0, high, jnp.where(ids == 1, middle, jnp.where(ids == 2, low, 0.0)))
    per_column = reached_ref.shape[0] // (width // 128)
    depth = state // per_column
    for piece in range(reached_ref.shape[0]):
        lanes = slice(128 * (piece // per_column), 128 * (piece // per_column) + 128)
        first = depth * (piece % per_column)
        reached_ref[piece, pl.ds(0, depth), :] = reached[first : first + depth, lanes]
        reached_ref[piece, pl.ds(depth, 8), :] = extra[:, lanes]


def local_states(x, x_taps, maps, maps_taps, raw, bias, decay_log, blocks, held):
    length, channels = x.shape
    heads = raw.shape[0]
    maps_width = maps.shape[1]
    width = 256
    columns = channels // width
    taps = x_taps.shape[0]
    state = maps_width // 2
    reached = (blocks, state * channels // (blocks * 128) + 8, 128)
    whole = lambda shape: pl.BlockSpec(shape, lambda i: (0,) * len(shape))
    return pl.pallas_call(
        functools.partial(state_kernel, heads, channels // heads, held),
        grid=(columns,),
        in_specs=[
            pl.BlockSpec((length, width), lambda i: (0, i)),
            pl.BlockSpec((taps, width), lambda i: (0, i)),
            whole((length, maps_width)),
            whole((taps, maps_width)),
            whole((heads, length)),
            whole((1, heads)),
            whole((1, heads)),
        ],
        out_specs=[
            pl.BlockSpec((length, width), lambda i: (0, i)),
            whole((length, maps_width)),
            whole((heads, length)),
            whole((heads, length)),
            whole((3 * heads, 128)),
            pl.BlockSpec((blocks // columns,) + reached[1:], lambda i: (i, 0, 0)),
        ],
        out_shape=[
            pltpu.HBM((length, channels), BF16),
            jax.ShapeDtypeStruct((length, maps_width), BF16),
            jax.ShapeDtypeStruct((heads, length), F32),
            jax.ShapeDtypeStruct((heads, length), F32),
            jax.ShapeDtypeStruct((3 * heads, 128), BF16),
            jax.ShapeDtypeStruct(reached, F32),
        ],
        scratch_shapes=[
            pltpu.VMEM((length + 8, width), F32),
            pltpu.VMEM((3 * heads, length), BF16),
            pltpu.VMEM((3 * heads, 128), BF16),
            pltpu.VMEM((length, width), BF16),
        ],
        compiler_params=params(),
        cost_estimate=pl.CostEstimate(
            flops=5_000_000_000, bytes_accessed=4_000_000, transcendentals=0
        ),
        name="local_states",
    )(x, x_taps, maps, maps_taps, raw, bias, decay_log)


def first_rows_kernel(
    head_dim,
    x_ref,
    maps_ref,
    halo_ref,
    x_taps_ref,
    maps_taps_ref,
    first_tail_ref,
    reached_ref,
    conv_in_ref,
    maps_conv_in_ref,
    conv_ref,
    maps_conv_ref,
    sent_ref,
    padded,
):
    held, channels = x_ref.shape
    maps_width = maps_ref.shape[1]
    leading = halo_ref.shape[0]
    state = maps_width // 2
    heads = first_tail_ref.shape[0] // 3
    padded[pl.ds(8 - leading, leading), :] = halo_ref[...].astype(F32)
    padded[pl.ds(8, held), :channels] = x_ref[...].astype(F32)
    padded[pl.ds(8, held), channels:] = maps_ref[...].astype(F32)
    taps = jnp.concatenate([x_taps_ref[...].astype(F32), maps_taps_ref[...].astype(F32)], axis=1)
    rows = silu(conv_rows(padded, taps, 0, held)).astype(BF16)
    conv_ref[...] = rows[:, :channels]
    maps_conv_ref[...] = rows[:, channels:]
    selector = head_selector(0, heads, head_dim, channels)
    tail = spread_heads(first_tail_ref[:, :held], selector)
    weighted = (tail * rows[:, :channels].astype(F32)).astype(BF16)
    more = lax.dot_general(
        rows[:, channels : channels + state],
        weighted,
        (((0,), (0,)), ((), ())),
        preferred_element_type=F32,
    )
    pieces = sent_ref.shape[0]
    per_column = pieces // (channels // 128)
    depth = state // per_column
    for piece in range(pieces):
        lanes = slice(128 * (piece // per_column), 128 * (piece // per_column) + 128)
        first = depth * (piece % per_column)
        sent_ref[piece] = jnp.concatenate(
            [
                reached_ref[piece, pl.ds(0, depth), :] + more[first : first + depth, lanes],
                reached_ref[piece, pl.ds(depth, 8), :],
            ],
            axis=0,
        ).astype(BF16)


def first_rows(x, maps, halo, x_taps, maps_taps, first_tail, reached, conv, maps_conv, held):
    heads = first_tail.shape[0] // 3
    channels, maps_width = x.shape[1], maps.shape[1]
    whole = lambda array: pl.BlockSpec(array.shape, lambda i: (0,) * array.ndim)
    head = lambda array: pl.BlockSpec((held, array.shape[1]), lambda i: (0, 0))
    near = pl.BlockSpec(memory_space=pltpu.VMEM)
    return pl.pallas_call(
        functools.partial(first_rows_kernel, channels // heads),
        grid=(1,),
        in_specs=[
            head(x),
            head(maps),
            near,
            whole(x_taps),
            whole(maps_taps),
            near,
            near,
            head(conv),
            head(maps_conv),
        ],
        out_specs=[head(conv), head(maps_conv), whole(reached)],
        out_shape=[
            pltpu.HBM(conv.shape, BF16),
            jax.ShapeDtypeStruct(maps_conv.shape, BF16),
            jax.ShapeDtypeStruct(reached.shape, BF16),
        ],
        scratch_shapes=[pltpu.VMEM((held + 8, channels + maps_width), F32)],
        input_output_aliases={7: 0, 8: 1},
        compiler_params=params(),
        name="first_rows",
    )(x, maps, halo, x_taps, maps_taps, first_tail, reached, conv, maps_conv)


def scan_kernel(got_ref, out_ref):
    blocks, rows, lanes = out_ref.shape
    running = jnp.zeros((rows, lanes), F32)
    for block in range(blocks):
        out_ref[block] = running.astype(BF16)
        if block < blocks - 1:
            piece = got_ref[block].astype(F32)
            factor = piece[rows : rows + 1] + (
                piece[rows + 1 : rows + 2] + piece[rows + 2 : rows + 3]
            )
            running = factor * running + piece[:rows]


def scan_blocks(got):
    blocks, rows, lanes = got.shape
    return pl.pallas_call(
        scan_kernel,
        out_shape=jax.ShapeDtypeStruct((blocks, rows - 8, lanes), BF16),
        compiler_params=params(),
        name="scan_blocks",
    )(got)


def local_kernel(
    head_dim, x_ref, maps_ref, z_ref, step_ref, total_ref, skip_ref, shown_ref, passed_ref, scores
):
    pair = pl.program_id(0)
    length, width = x_ref.shape
    state = maps_ref.shape[1] // 2
    per_step = width // head_dim
    tile = 128

    @pl.when(pair == 0)
    def _():
        scores[...] = lax.dot_general(
            maps_ref[:, state:],
            maps_ref[:, :state],
            (((1,), (1,)), ((), ())),
            preferred_element_type=F32,
        )

    later = lax.broadcasted_iota(jnp.int32, (tile, tile), 0)
    earlier = lax.broadcasted_iota(jnp.int32, (tile, tile), 1)
    causal = later >= earlier
    lanes = lax.broadcasted_iota(jnp.int32, (tile, width), 1)
    totals = [total_ref[pl.ds(pair * per_step + head, 1), :] for head in range(per_step)]
    steps = [step_ref[pl.ds(pair * per_step + head, 1), :] for head in range(per_step)]
    skip = skip_ref[pair * per_step]
    for head in range(1, per_step):
        skip = jnp.where(lanes >= head * head_dim, skip_ref[pair * per_step + head], skip)
    for start in range(0, length, tile):
        outs = []
        outer = None
        for head in range(per_step):
            columns = jnp.broadcast_to(totals[head][:, start : start + tile], (tile, tile)).T
            weights = []
            for source in range(0, start + tile, tile):
                spread = totals[head][:, source : source + tile] - columns
                if source == start:
                    spread = jnp.where(causal, spread, -1e30)
                part = jnp.exp(spread) * scores[pl.ds(start, tile), pl.ds(source, tile)]
                part = part * steps[head][:, source : source + tile]
                weights.append(part.astype(BF16))
            weights = weights[0] if len(weights) == 1 else jnp.concatenate(weights, axis=1)
            outs.append(
                jnp.dot(
                    weights,
                    x_ref[pl.ds(0, start + tile), pl.ds(head * head_dim, head_dim)],
                    preferred_element_type=F32,
                )
            )
            fade = jnp.exp(-columns)
            outer = fade if outer is None else jnp.where(lanes >= head * head_dim, fade, outer)
        values = x_ref[pl.ds(start, tile), :].astype(F32)
        gate = silu(z_ref[pl.ds(start, tile), :].astype(F32))
        out = jnp.concatenate(outs, axis=1) + skip * values
        shown_ref[pl.ds(start, tile), :] = (out * gate).astype(BF16)
        passed_ref[pl.ds(start, tile), :] = (outer * gate).astype(BF16)


def local_outputs(x_conv, maps_conv, z, step_rows, total_rows, skip, head_dim):
    length, channels = x_conv.shape
    width = 128
    columns = channels // width
    heads = channels // head_dim
    maps_width = maps_conv.shape[1]
    block = pl.BlockSpec((length, width), lambda i: (0, i))
    row_block = pl.BlockSpec((heads, length), lambda i: (0, 0))
    return pl.pallas_call(
        functools.partial(local_kernel, head_dim),
        grid=(columns,),
        in_specs=[
            block,
            pl.BlockSpec((length, maps_width), lambda i: (0, 0)),
            block,
            row_block,
            row_block,
            pl.BlockSpec(memory_space=pltpu.SMEM),
        ],
        out_specs=[block, block],
        out_shape=[jax.ShapeDtypeStruct((length, channels), BF16)] * 2,
        scratch_shapes=[pltpu.VMEM((length, length), F32)],
        compiler_params=params(),
        cost_estimate=pl.CostEstimate(
            flops=8_000_000_000, bytes_accessed=6_000_000, transcendentals=0
        ),
        name="local_outputs",
    )(x_conv, maps_conv, z, step_rows, total_rows, skip)


def fetches(sources, targets, columns, arrived):
    pieces = 4
    copies = []
    for index, (source, target) in enumerate(zip(sources, targets)):
        depth = target.shape[0] // pieces
        for piece in range(pieces):
            rows = pl.ds(piece * depth, depth)
            copies.append(
                pltpu.make_async_copy(
                    source.at[rows, columns],
                    target.at[rows, :],
                    arrived.at[index * pieces + piece],
                )
            )
    return copies


def norm_kernel(other, carried_ref, maps_ref, shown_ref, passed_ref, gain_ref, *rest):
    copies = []
    if other:
        out_ref, entering = rest
    else:
        sources, out_ref, targets, (entering, arrived) = rest[:2], rest[2], rest[3:5], rest[5:]
        copies = fetches(sources, targets, pl.ds(0, targets[0].shape[1]), arrived)
    for copy in copies:
        copy.start()
    state, channels = entering.shape
    pieces, depth, lanes = carried_ref.shape
    per_column = state // depth
    for piece in range(pieces):
        entering[
            pl.ds(depth * (piece % per_column), depth),
            pl.ds(lanes * (piece // per_column), lanes),
        ] = carried_ref[piece]
    ring = len(TURNS)
    size = out_ref.shape[0] // ring
    place = lax.axis_index("tp")
    across, core = place // 2, lax.rem(place, 2)
    if other:
        core = 1 - core
    for turn, ahead in enumerate(TURNS):
        pick = 2 * lax.rem(across + ahead, ring) + core
        rows = pl.ds(pl.multiple_of(pick * size, size), size)
        carry = jnp.dot(maps_ref[rows, state:], entering[...], preferred_element_type=F32)
        gated = shown_ref[rows, :].astype(F32) + carry * passed_ref[rows, :].astype(F32)
        scale = lax.rsqrt(jnp.mean(gated * gated, axis=1, keepdims=True) + 1e-05)
        out_ref[pl.ds(size * turn, size), :] = (gated * scale * gain_ref[...]).astype(BF16)
    for copy in copies:
        copy.wait()


def normed_rows(other, carried, maps_conv, shown, passed, gain, weights, name):
    length, channels = shown.shape
    state = maps_conv.shape[1] // 2
    near = pl.BlockSpec(memory_space=pltpu.VMEM)
    far = pl.BlockSpec(memory_space=pltpu.HBM)
    normed = jax.ShapeDtypeStruct((length // 2, channels), BF16)
    scratch = [pltpu.VMEM((state, channels), BF16)]
    fetched = []
    if not other:
        fetched = [jax.ShapeDtypeStruct((w.shape[0], w.shape[1] // 2), BF16) for w in weights]
        scratch.append(pltpu.SemaphoreType.DMA((8,)))
    return pl.pallas_call(
        functools.partial(norm_kernel, other),
        in_specs=[near] * 5 + [far] * len(weights),
        out_specs=[near] * (1 + len(fetched)),
        scratch_shapes=scratch,
        out_shape=[normed] + fetched,
        compiler_params=params(),
        cost_estimate=pl.CostEstimate(
            flops=1_000_000_000, bytes_accessed=3_000_000, transcendentals=0
        ),
        name=name,
    )(carried, maps_conv, shown, passed, gain, *[far_memory(weight) for weight in weights])


def project_near_kernel(own_ref, other_ref, own_weight_ref, other_weight_ref, *out_refs):
    rows, columns = out_refs[0].shape
    width = 512
    for start in range(0, columns, width):
        lanes = pl.ds(start, width)
        product = jnp.dot(own_ref[...], own_weight_ref[:, lanes], preferred_element_type=F32)
        product = product + jnp.dot(
            other_ref[...], other_weight_ref[:, lanes], preferred_element_type=F32
        )
        for index, out_ref in enumerate(out_refs):
            piece = product[rows * index : rows * (index + 1)]
            out_ref[:, lanes] = piece.astype(out_ref.dtype)


def project_far_kernel(own_ref, other_ref, own_weight_ref, other_weight_ref, *rest):
    out_refs, (own_near, other_near, total, arrived) = rest[:4], rest[4:]
    rows, columns = out_refs[0].shape
    width = 512
    copies = fetches(
        (own_weight_ref, other_weight_ref),
        (own_near, other_near),
        pl.ds(columns, columns),
        arrived,
    )
    half = len(copies) // 2
    for copy in copies:
        copy.start()
    for copy in copies[:half]:
        copy.wait()
    for start in range(0, columns, width):
        lanes = pl.ds(start, width)
        total[:, lanes] = jnp.dot(
            own_ref[...], own_near[:, lanes], preferred_element_type=F32
        )
    for copy in copies[half:]:
        copy.wait()
    for start in range(0, columns, width):
        lanes = pl.ds(start, width)
        product = total[:, lanes] + jnp.dot(
            other_ref[...], other_near[:, lanes], preferred_element_type=F32
        )
        for index, out_ref in enumerate(out_refs):
            piece = product[rows * index : rows * (index + 1)]
            out_ref[:, lanes] = piece.astype(out_ref.dtype)


def project(own, other, own_weight, other_weight, columns, name):
    count, depth = own.shape
    near = pl.BlockSpec(memory_space=pltpu.VMEM)
    far = own_weight.shape[1] > columns
    weight_spec = pl.BlockSpec(memory_space=pltpu.HBM) if far else near
    weights = [own_weight, other_weight]
    return pl.pallas_call(
        project_far_kernel if far else project_near_kernel,
        in_specs=[near, near, weight_spec, weight_spec],
        out_specs=[near] * 4,
        out_shape=[jax.ShapeDtypeStruct((count // 4, columns), BF16)] * 4,
        scratch_shapes=[
            pltpu.VMEM((depth, columns), BF16),
            pltpu.VMEM((depth, columns), BF16),
            pltpu.VMEM((count, columns), F32),
            pltpu.SemaphoreType.DMA((8,)),
        ]
        if far
        else [],
        compiler_params=params(),
        cost_estimate=pl.CostEstimate(
            flops=4 * count * depth * columns, bytes_accessed=9_000_000, transcendentals=0
        ),
        name=name,
    )(own, other, *([far_memory(weight) for weight in weights] if far else weights))


def on_device(
    x_inputs,
    state_maps,
    z_gate,
    step_raw,
    step_bias,
    decay_log,
    skip_gain,
    x_filter,
    state_filter,
    norm_gain,
    out_weight,
):
    length, channels = x_inputs.shape
    leading = x_filter.shape[0] - 1
    heads = step_raw.shape[1]
    head_dim = channels // heads
    blocks = lax.axis_size("ctx")
    members = lax.axis_size("tp")
    ring = members // 2

    def core_swap(value):
        return lax.ppermute(value, "tp", [(i, i ^ 1) for i in range(members)])

    def along(value, steps):
        pairs = [
            (2 * y + c, 2 * ((y + steps) % ring) + c) for y in range(ring) for c in range(2)
        ]
        return lax.ppermute(value, "tp", pairs)

    ends = jnp.concatenate([x_inputs[length - leading :], state_maps[length - leading :]], axis=1)
    halo = shifted(ends, "ctx", 1)
    x_inputs, state_maps = far_memory(x_inputs), far_memory(state_maps)
    x_filter, state_filter = far_memory(x_filter), far_memory(state_filter)
    held = 16
    conv, maps_conv, step, total, first_tail, reached = local_states(
        x_inputs,
        x_filter,
        state_maps,
        state_filter,
        far_memory(step_raw.T),
        far_memory(step_bias[None]),
        far_memory(decay_log[None]),
        blocks,
        held,
    )
    other_weight = core_swap(lax.optimization_barrier((out_weight, halo, first_tail))[0])
    x_conv, maps_conv, sent = first_rows(
        x_inputs,
        state_maps,
        halo,
        x_filter,
        state_filter,
        first_tail,
        reached,
        conv,
        maps_conv,
        held,
    )
    got = lax.all_to_all(sent, "ctx", 0, 0, tiled=True)
    shown, passed = local_outputs(
        x_conv,
        maps_conv,
        far_memory(z_gate),
        step,
        total,
        skip_gain,
        head_dim,
    )
    got, shown, passed = lax.optimization_barrier((got, shown, passed))
    entering = scan_blocks(got)
    carried = lax.all_to_all(entering, "ctx", 0, 0, tiled=True)

    gain = norm_gain[None]
    weights = (out_weight, other_weight)
    (give,) = normed_rows(True, carried, maps_conv, shown, passed, gain, (), "give_rows")
    taken = core_swap(give)
    keep, own_left, other_left = normed_rows(
        False, carried, maps_conv, shown, passed, gain, weights, "keep_rows"
    )
    columns = own_left.shape[1]
    far_a, up_a, down_a, own_a = project(keep, taken, own_left, other_left, columns, "left_half")
    far_b, up_b, down_b, own_b = project(
        keep, taken, out_weight, other_weight, columns, "right_half"
    )

    def added(*values):
        return functools.reduce(lambda a, b: a + b, [v.astype(F32) for v in values]).astype(BF16)

    relay_a = along(far_a, 1)
    from_above_a = along(down_a, -1)
    relay_b = along(far_b, -1)
    from_below_b = along(up_b, 1)
    from_below_a = along(added(up_a, relay_a), 1)
    from_above_b = along(added(down_b, relay_b), -1)
    return jnp.concatenate(
        [added(own_a, from_above_a, from_below_a), added(own_b, from_above_b, from_below_b)], axis=1
    )


def solution(mesh):
    return jax.shard_map(
        on_device,
        mesh=mesh,
        in_specs=(
            P("ctx", "tp"),
            P("ctx", "tp"),
            P("ctx", "tp"),
            P("ctx", "tp"),
            P("tp"),
            P("tp"),
            P("tp"),
            P(None, "tp"),
            P(None, "tp"),
            P("tp"),
            P("tp", None),
        ),
        out_specs=P(("ctx", "tp"), None),
        check_vma=False,
    )
```

```python
import functools

import jax
import jax.numpy as jnp
from jax import lax
from jax.experimental import pallas as pl
from jax.experimental.pallas import tpu as pltpu
from jax.sharding import PartitionSpec as P

BF16 = jnp.bfloat16
F32 = jnp.float32
VMEM_LIMIT = 16 * 1024 * 1024
TURNS = (2, 1, 3, 0)


def far_memory(value):
    return pltpu.with_memory_space_constraint(value, pltpu.HBM)


def params(**more):
    return pltpu.CompilerParams(vmem_limit_bytes=VMEM_LIMIT, **more)


def shifted(value, axis, steps):
    count = lax.axis_size(axis)
    leading, last = (max(0, -steps), min(count, count - steps))
    return lax.ppermute(value, axis, [(source, source + steps) for source in range(leading, last)])


def three_parts(value):
    high = value.astype(BF16)
    rest = value - high.astype(F32)
    middle = rest.astype(BF16)
    low = (rest - middle.astype(F32)).astype(BF16)
    return high, middle, low


def packed_parts(value):
    high, middle, low = three_parts(value)
    wide = [high.astype(F32), middle.astype(F32), low.astype(F32)]
    return jnp.concatenate(wide, axis=0).astype(BF16)


def head_selector(first_head, heads, head_dim, width):
    rows = lax.broadcasted_iota(jnp.int32, (3 * heads, width), 0)
    lanes = lax.broadcasted_iota(jnp.int32, (3 * heads, width), 1)
    return (rows % heads == first_head + lanes // head_dim).astype(F32).astype(BF16)


def spread_heads(parts, selector):
    return lax.dot_general(
        parts, selector, (((0,), (0,)), ((), ())), preferred_element_type=F32
    )


def silu(value):
    return value / (1.0 + jnp.exp(-value))


def conv_rows(padded, taps, start, rows):
    count = taps.shape[0]
    columns = []
    for column in range(taps.shape[1] // 128):
        total = None
        for offset in range(count):
            first = 8 - (count - 1) + offset + start
            weight = taps[offset : offset + 1, 128 * column : 128 * column + 128]
            term = weight * padded[column, pl.ds(first, rows), :]
            total = term if total is None else total + term
        columns.append(total)
    return columns[0] if len(columns) == 1 else jnp.concatenate(columns, axis=1)


def state_kernel(
    heads,
    head_dim,
    held,
    x_ref,
    x_taps_ref,
    maps_ref,
    maps_taps_ref,
    raw_ref,
    bias_ref,
    decay_ref,
    conv_ref,
    maps_conv_ref,
    step_ref,
    total_ref,
    first_tail_ref,
    reached_ref,
    padded,
    tail_parts,
    end_parts,
    weighted,
):
    column = pl.program_id(0)
    length, width = x_ref.shape
    tile = 128
    state = maps_ref.shape[1] // 2

    def fill(source):
        for column in range(source.shape[1] // 128):
            lanes = pl.ds(128 * column, 128)
            padded[column, pl.ds(0, 8), :] = jnp.zeros((8, 128), F32)
            for start in range(0, length, tile):
                rows = pl.ds(8 + start, tile)
                padded[column, rows, :] = source[pl.ds(start, tile), lanes].astype(F32)

    @pl.when(column == 0)
    def _():
        row_ids = lax.broadcasted_iota(jnp.int32, (heads, heads), 0)
        col_ids = lax.broadcasted_iota(jnp.int32, (heads, heads), 1)

        def as_column(ref):
            spread = jnp.where(row_ids == col_ids, ref[...], 0.0)
            return jnp.sum(spread, axis=1, keepdims=True)

        step = jnp.log1p(jnp.exp(raw_ref[...] + as_column(bias_ref)))
        step_ref[...] = step
        rate = step * jnp.exp(as_column(decay_ref))
        piece = 128
        source = lax.broadcasted_iota(jnp.int32, (piece, piece), 0)
        target = lax.broadcasted_iota(jnp.int32, (piece, piece), 1)
        triangle = (source <= target).astype(F32).astype(BF16)
        before = jnp.zeros((heads, 1), F32)
        for start in range(0, length, piece):
            parts = three_parts(rate[:, start : start + piece])
            sums = [jnp.dot(part, triangle, preferred_element_type=F32) for part in parts]
            block = sums[0] + (sums[1] + sums[2]) + before
            total_ref[:, pl.ds(start, piece)] = block
            before = block[:, piece - 1 : piece]
        tail_parts[...] = packed_parts(jnp.exp(total_ref[...] - before) * step)
        end_parts[...] = packed_parts(jnp.broadcast_to(jnp.exp(-before), (heads, 128)))
        first_tail_ref[...] = tail_parts[:, :128]
        fill(maps_ref)
        taps = maps_taps_ref[...].astype(F32)
        for start in range(0, length, tile):
            rows = silu(conv_rows(padded, taps, start, tile))
            maps_conv_ref[pl.ds(start, tile), :] = rows.astype(BF16)

    fill(x_ref)
    taps = x_taps_ref[...].astype(F32)
    selector = head_selector(column * (width // head_dim), heads, head_dim, width)
    for start in range(0, length, tile):
        rows = silu(conv_rows(padded, taps, start, tile)).astype(BF16)
        conv_ref[pl.ds(start, tile), :] = rows
        tail = spread_heads(tail_parts[:, start : start + tile], selector)
        scaled = tail * rows.astype(F32)
        if start == 0:
            ids = lax.broadcasted_iota(jnp.int32, scaled.shape, 0)
            scaled = jnp.where(ids >= held, scaled, 0.0)
        weighted[pl.ds(start, tile), :] = scaled.astype(BF16)
    reached = lax.dot_general(
        maps_conv_ref[:, :state],
        weighted[...],
        (((0,), (0,)), ((), ())),
        preferred_element_type=F32,
    )
    factor = spread_heads(end_parts[:, :8], selector)
    high, middle, low = [part.astype(F32) for part in three_parts(factor)]
    ids = lax.broadcasted_iota(jnp.int32, factor.shape, 0)
    extra = jnp.where(ids == 0, high, jnp.where(ids == 1, middle, jnp.where(ids == 2, low, 0.0)))
    per_column = reached_ref.shape[0] // (width // 128)
    depth = state // per_column
    for piece in range(reached_ref.shape[0]):
        lanes = slice(128 * (piece // per_column), 128 * (piece // per_column) + 128)
        first = depth * (piece % per_column)
        reached_ref[piece, pl.ds(0, depth), :] = reached[first : first + depth, lanes]
        reached_ref[piece, pl.ds(depth, 8), :] = extra[:, lanes]


def local_states(x, x_taps, maps, maps_taps, raw, bias, decay_log, blocks, held):
    length, channels = x.shape
    heads = raw.shape[0]
    maps_width = maps.shape[1]
    width = 512
    columns = channels // width
    taps = x_taps.shape[0]
    state = maps_width // 2
    reached = (blocks, state * channels // (blocks * 128) + 8, 128)
    whole = lambda shape: pl.BlockSpec(shape, lambda i: (0,) * len(shape))
    return pl.pallas_call(
        functools.partial(state_kernel, heads, channels // heads, held),
        grid=(columns,),
        in_specs=[
            pl.BlockSpec((length, width), lambda i: (0, i)),
            pl.BlockSpec((taps, width), lambda i: (0, i)),
            whole((length, maps_width)),
            whole((taps, maps_width)),
            whole((heads, length)),
            whole((1, heads)),
            whole((1, heads)),
        ],
        out_specs=[
            pl.BlockSpec((length, width), lambda i: (0, i)),
            whole((length, maps_width)),
            whole((heads, length)),
            whole((heads, length)),
            whole((3 * heads, 128)),
            pl.BlockSpec((blocks // columns,) + reached[1:], lambda i: (i, 0, 0)),
        ],
        out_shape=[
            pltpu.HBM((length, channels), BF16),
            jax.ShapeDtypeStruct((length, maps_width), BF16),
            jax.ShapeDtypeStruct((heads, length), F32),
            jax.ShapeDtypeStruct((heads, length), F32),
            jax.ShapeDtypeStruct((3 * heads, 128), BF16),
            jax.ShapeDtypeStruct(reached, F32),
        ],
        scratch_shapes=[
            pltpu.VMEM((width // 128, length + 8, 128), F32),
            pltpu.VMEM((3 * heads, length), BF16),
            pltpu.VMEM((3 * heads, 128), BF16),
            pltpu.VMEM((length, width), BF16),
        ],
        compiler_params=params(),
        cost_estimate=pl.CostEstimate(
            flops=5_000_000_000, bytes_accessed=4_000_000, transcendentals=0
        ),
        name="local_states",
    )(x, x_taps, maps, maps_taps, raw, bias, decay_log)


def first_rows_kernel(
    head_dim,
    x_ref,
    maps_ref,
    halo_ref,
    x_taps_ref,
    maps_taps_ref,
    first_tail_ref,
    reached_ref,
    conv_in_ref,
    maps_conv_in_ref,
    conv_ref,
    maps_conv_ref,
    sent_ref,
    padded,
):
    held, channels = x_ref.shape
    maps_width = maps_ref.shape[1]
    leading = halo_ref.shape[0]
    state = maps_width // 2
    heads = first_tail_ref.shape[0] // 3
    for column in range(padded.shape[0]):
        lanes = pl.ds(128 * column, 128)
        padded[column, pl.ds(8 - leading, leading), :] = halo_ref[:, lanes].astype(F32)
        source, first = (x_ref, 0) if 128 * column < channels else (maps_ref, channels)
        lanes = pl.ds(128 * column - first, 128)
        padded[column, pl.ds(8, held), :] = source[:, lanes].astype(F32)
    taps = jnp.concatenate([x_taps_ref[...].astype(F32), maps_taps_ref[...].astype(F32)], axis=1)
    rows = silu(conv_rows(padded, taps, 0, held)).astype(BF16)
    conv_ref[...] = rows[:, :channels]
    maps_conv_ref[...] = rows[:, channels:]
    selector = head_selector(0, heads, head_dim, channels)
    tail = spread_heads(first_tail_ref[:, :held], selector)
    weighted = (tail * rows[:, :channels].astype(F32)).astype(BF16)
    more = lax.dot_general(
        rows[:, channels : channels + state],
        weighted,
        (((0,), (0,)), ((), ())),
        preferred_element_type=F32,
    )
    pieces = sent_ref.shape[0]
    per_column = pieces // (channels // 128)
    depth = state // per_column
    for piece in range(pieces):
        lanes = slice(128 * (piece // per_column), 128 * (piece // per_column) + 128)
        first = depth * (piece % per_column)
        sent_ref[piece] = jnp.concatenate(
            [
                reached_ref[piece, pl.ds(0, depth), :] + more[first : first + depth, lanes],
                reached_ref[piece, pl.ds(depth, 8), :],
            ],
            axis=0,
        ).astype(BF16)


def first_rows(x, maps, halo, x_taps, maps_taps, first_tail, reached, conv, maps_conv, held):
    heads = first_tail.shape[0] // 3
    channels, maps_width = x.shape[1], maps.shape[1]
    whole = lambda array: pl.BlockSpec(array.shape, lambda i: (0,) * array.ndim)
    head = lambda array: pl.BlockSpec((held, array.shape[1]), lambda i: (0, 0))
    near = pl.BlockSpec(memory_space=pltpu.VMEM)
    return pl.pallas_call(
        functools.partial(first_rows_kernel, channels // heads),
        grid=(1,),
        in_specs=[
            head(x),
            head(maps),
            near,
            whole(x_taps),
            whole(maps_taps),
            near,
            near,
            head(conv),
            head(maps_conv),
        ],
        out_specs=[head(conv), head(maps_conv), whole(reached)],
        out_shape=[
            pltpu.HBM(conv.shape, BF16),
            jax.ShapeDtypeStruct(maps_conv.shape, BF16),
            jax.ShapeDtypeStruct(reached.shape, BF16),
        ],
        scratch_shapes=[pltpu.VMEM(((channels + maps_width) // 128, held + 8, 128), F32)],
        input_output_aliases={7: 0, 8: 1},
        compiler_params=params(),
        name="first_rows",
    )(x, maps, halo, x_taps, maps_taps, first_tail, reached, conv, maps_conv)


def scan_kernel(got_ref, out_ref):
    blocks, rows, lanes = out_ref.shape
    running = jnp.zeros((rows, lanes), F32)
    for block in range(blocks):
        out_ref[block] = running.astype(BF16)
        if block < blocks - 1:
            piece = got_ref[block].astype(F32)
            factor = piece[rows : rows + 1] + (
                piece[rows + 1 : rows + 2] + piece[rows + 2 : rows + 3]
            )
            running = factor * running + piece[:rows]


def scan_blocks(got):
    blocks, rows, lanes = got.shape
    return pl.pallas_call(
        scan_kernel,
        out_shape=jax.ShapeDtypeStruct((blocks, rows - 8, lanes), BF16),
        compiler_params=params(),
        name="scan_blocks",
    )(got)


def local_kernel(
    head_dim, x_ref, maps_ref, z_ref, step_ref, total_ref, skip_ref, shown_ref, passed_ref, scores
):
    pair = pl.program_id(0)
    length, width = x_ref.shape
    state = maps_ref.shape[1] // 2
    per_step = width // head_dim
    tile = 128

    @pl.when(pair == 0)
    def _():
        scores[...] = lax.dot_general(
            maps_ref[:, state:],
            maps_ref[:, :state],
            (((1,), (1,)), ((), ())),
            preferred_element_type=F32,
        )

    later = lax.broadcasted_iota(jnp.int32, (tile, tile), 0)
    earlier = lax.broadcasted_iota(jnp.int32, (tile, tile), 1)
    causal = later >= earlier
    lanes = lax.broadcasted_iota(jnp.int32, (tile, width), 1)
    totals = [total_ref[pl.ds(pair * per_step + head, 1), :] for head in range(per_step)]
    steps = [step_ref[pl.ds(pair * per_step + head, 1), :] for head in range(per_step)]
    skip = skip_ref[pair * per_step]
    for head in range(1, per_step):
        skip = jnp.where(lanes >= head * head_dim, skip_ref[pair * per_step + head], skip)
    for start in range(0, length, tile):
        outs = []
        outer = None
        for head in range(per_step):
            columns = jnp.broadcast_to(totals[head][:, start : start + tile], (tile, tile)).T
            weights = []
            for source in range(0, start + tile, tile):
                spread = totals[head][:, source : source + tile] - columns
                if source == start:
                    spread = jnp.where(causal, spread, -1e30)
                part = jnp.exp(spread) * scores[pl.ds(start, tile), pl.ds(source, tile)]
                part = part * steps[head][:, source : source + tile]
                weights.append(part.astype(BF16))
            weights = weights[0] if len(weights) == 1 else jnp.concatenate(weights, axis=1)
            outs.append(
                jnp.dot(
                    weights,
                    x_ref[pl.ds(0, start + tile), pl.ds(head * head_dim, head_dim)],
                    preferred_element_type=F32,
                )
            )
            fade = jnp.exp(-columns)
            outer = fade if outer is None else jnp.where(lanes >= head * head_dim, fade, outer)
        values = x_ref[pl.ds(start, tile), :].astype(F32)
        gate = silu(z_ref[pl.ds(start, tile), :].astype(F32))
        out = jnp.concatenate(outs, axis=1) + skip * values
        shown_ref[pl.ds(start, tile), :] = (out * gate).astype(BF16)
        passed_ref[pl.ds(start, tile), :] = (outer * gate).astype(BF16)


def local_outputs(x_conv, maps_conv, z, step_rows, total_rows, skip, head_dim):
    length, channels = x_conv.shape
    width = 128
    columns = channels // width
    heads = channels // head_dim
    maps_width = maps_conv.shape[1]
    block = pl.BlockSpec((length, width), lambda i: (0, i))
    row_block = pl.BlockSpec((heads, length), lambda i: (0, 0))
    return pl.pallas_call(
        functools.partial(local_kernel, head_dim),
        grid=(columns,),
        in_specs=[
            block,
            pl.BlockSpec((length, maps_width), lambda i: (0, 0)),
            block,
            row_block,
            row_block,
            pl.BlockSpec(memory_space=pltpu.SMEM),
        ],
        out_specs=[block, block],
        out_shape=[jax.ShapeDtypeStruct((length, channels), BF16)] * 2,
        scratch_shapes=[pltpu.VMEM((length, length), F32)],
        compiler_params=params(),
        cost_estimate=pl.CostEstimate(
            flops=8_000_000_000, bytes_accessed=6_000_000, transcendentals=0
        ),
        name="local_outputs",
    )(x_conv, maps_conv, z, step_rows, total_rows, skip)


def fetches(sources, targets, columns, arrived):
    pieces = 4
    copies = []
    for index, (source, target) in enumerate(zip(sources, targets)):
        depth = target.shape[0] // pieces
        for piece in range(pieces):
            rows = pl.ds(piece * depth, depth)
            copies.append(
                pltpu.make_async_copy(
                    source.at[rows, columns],
                    target.at[rows, :],
                    arrived.at[index * pieces + piece],
                )
            )
    return copies


def norm_kernel(other, carried_ref, maps_ref, shown_ref, passed_ref, gain_ref, *rest):
    copies = []
    if other:
        out_ref, entering = rest
    else:
        sources, out_ref, targets, (entering, arrived) = rest[:2], rest[2], rest[3:5], rest[5:]
        copies = fetches(sources, targets, pl.ds(0, targets[0].shape[1]), arrived)
    for copy in copies:
        copy.start()
    state, channels = entering.shape
    pieces, depth, lanes = carried_ref.shape
    per_column = state // depth
    for piece in range(pieces):
        entering[
            pl.ds(depth * (piece % per_column), depth),
            pl.ds(lanes * (piece // per_column), lanes),
        ] = carried_ref[piece]
    ring = len(TURNS)
    size = out_ref.shape[0] // ring
    place = lax.axis_index("tp")
    across, core = place // 2, lax.rem(place, 2)
    if other:
        core = 1 - core
    for turn, ahead in enumerate(TURNS):
        pick = 2 * lax.rem(across + ahead, ring) + core
        rows = pl.ds(pl.multiple_of(pick * size, size), size)
        carry = jnp.dot(maps_ref[rows, state:], entering[...], preferred_element_type=F32)
        gated = shown_ref[rows, :].astype(F32) + carry * passed_ref[rows, :].astype(F32)
        scale = lax.rsqrt(jnp.mean(gated * gated, axis=1, keepdims=True) + 1e-05)
        out_ref[pl.ds(size * turn, size), :] = (gated * scale * gain_ref[...]).astype(BF16)
    for copy in copies:
        copy.wait()


def normed_rows(other, carried, maps_conv, shown, passed, gain, weights, name):
    length, channels = shown.shape
    state = maps_conv.shape[1] // 2
    near = pl.BlockSpec(memory_space=pltpu.VMEM)
    far = pl.BlockSpec(memory_space=pltpu.HBM)
    normed = jax.ShapeDtypeStruct((length // 2, channels), BF16)
    scratch = [pltpu.VMEM((state, channels), BF16)]
    fetched = []
    if not other:
        fetched = [jax.ShapeDtypeStruct((w.shape[0], w.shape[1] // 2), BF16) for w in weights]
        scratch.append(pltpu.SemaphoreType.DMA((8,)))
    return pl.pallas_call(
        functools.partial(norm_kernel, other),
        in_specs=[near] * 5 + [far] * len(weights),
        out_specs=[near] * (1 + len(fetched)),
        scratch_shapes=scratch,
        out_shape=[normed] + fetched,
        compiler_params=params(),
        cost_estimate=pl.CostEstimate(
            flops=1_000_000_000, bytes_accessed=3_000_000, transcendentals=0
        ),
        name=name,
    )(carried, maps_conv, shown, passed, gain, *[far_memory(weight) for weight in weights])


def project_near_kernel(own_ref, other_ref, own_weight_ref, other_weight_ref, *out_refs):
    rows, columns = out_refs[0].shape
    width = 512
    for start in range(0, columns, width):
        lanes = pl.ds(start, width)
        product = jnp.dot(own_ref[...], own_weight_ref[:, lanes], preferred_element_type=F32)
        product = product + jnp.dot(
            other_ref[...], other_weight_ref[:, lanes], preferred_element_type=F32
        )
        for index, out_ref in enumerate(out_refs):
            piece = product[rows * index : rows * (index + 1)]
            out_ref[:, lanes] = piece.astype(out_ref.dtype)


def project_far_kernel(own_ref, other_ref, own_weight_ref, other_weight_ref, *rest):
    out_refs, (own_near, other_near, total, arrived) = rest[:4], rest[4:]
    rows, columns = out_refs[0].shape
    width = 512
    copies = fetches(
        (own_weight_ref, other_weight_ref),
        (own_near, other_near),
        pl.ds(columns, columns),
        arrived,
    )
    half = len(copies) // 2
    for copy in copies:
        copy.start()
    for copy in copies[:half]:
        copy.wait()
    for start in range(0, columns, width):
        lanes = pl.ds(start, width)
        total[:, lanes] = jnp.dot(
            own_ref[...], own_near[:, lanes], preferred_element_type=F32
        )
    for copy in copies[half:]:
        copy.wait()
    for start in range(0, columns, width):
        lanes = pl.ds(start, width)
        product = total[:, lanes] + jnp.dot(
            other_ref[...], other_near[:, lanes], preferred_element_type=F32
        )
        for index, out_ref in enumerate(out_refs):
            piece = product[rows * index : rows * (index + 1)]
            out_ref[:, lanes] = piece.astype(out_ref.dtype)


def project(own, other, own_weight, other_weight, columns, name):
    count, depth = own.shape
    near = pl.BlockSpec(memory_space=pltpu.VMEM)
    far = own_weight.shape[1] > columns
    weight_spec = pl.BlockSpec(memory_space=pltpu.HBM) if far else near
    weights = [own_weight, other_weight]
    return pl.pallas_call(
        project_far_kernel if far else project_near_kernel,
        in_specs=[near, near, weight_spec, weight_spec],
        out_specs=[near] * 4,
        out_shape=[jax.ShapeDtypeStruct((count // 4, columns), BF16)] * 4,
        scratch_shapes=[
            pltpu.VMEM((depth, columns), BF16),
            pltpu.VMEM((depth, columns), BF16),
            pltpu.VMEM((count, columns), F32),
            pltpu.SemaphoreType.DMA((8,)),
        ]
        if far
        else [],
        compiler_params=params(),
        cost_estimate=pl.CostEstimate(
            flops=4 * count * depth * columns, bytes_accessed=9_000_000, transcendentals=0
        ),
        name=name,
    )(own, other, *([far_memory(weight) for weight in weights] if far else weights))


def on_device(
    x_inputs,
    state_maps,
    z_gate,
    step_raw,
    step_bias,
    decay_log,
    skip_gain,
    x_filter,
    state_filter,
    norm_gain,
    out_weight,
):
    length, channels = x_inputs.shape
    leading = x_filter.shape[0] - 1
    heads = step_raw.shape[1]
    head_dim = channels // heads
    blocks = lax.axis_size("ctx")
    members = lax.axis_size("tp")
    ring = members // 2

    def core_swap(value):
        return lax.ppermute(value, "tp", [(i, i ^ 1) for i in range(members)])

    def along(value, steps):
        pairs = [
            (2 * y + c, 2 * ((y + steps) % ring) + c) for y in range(ring) for c in range(2)
        ]
        return lax.ppermute(value, "tp", pairs)

    ends = jnp.concatenate([x_inputs[length - leading :], state_maps[length - leading :]], axis=1)
    halo = shifted(ends, "ctx", 1)
    x_inputs, state_maps = far_memory(x_inputs), far_memory(state_maps)
    x_filter, state_filter = far_memory(x_filter), far_memory(state_filter)
    held = 16
    conv, maps_conv, step, total, first_tail, reached = local_states(
        x_inputs,
        x_filter,
        state_maps,
        state_filter,
        far_memory(step_raw.T),
        far_memory(step_bias[None]),
        far_memory(decay_log[None]),
        blocks,
        held,
    )
    other_weight = core_swap(lax.optimization_barrier((out_weight, halo, first_tail))[0])
    x_conv, maps_conv, sent = first_rows(
        x_inputs,
        state_maps,
        halo,
        x_filter,
        state_filter,
        first_tail,
        reached,
        conv,
        maps_conv,
        held,
    )
    got = lax.all_to_all(sent, "ctx", 0, 0, tiled=True)
    shown, passed = local_outputs(
        x_conv,
        maps_conv,
        far_memory(z_gate),
        step,
        total,
        skip_gain,
        head_dim,
    )
    got, shown, passed = lax.optimization_barrier((got, shown, passed))
    entering = scan_blocks(got)
    carried = lax.all_to_all(entering, "ctx", 0, 0, tiled=True)

    gain = norm_gain[None]
    weights = (out_weight, other_weight)
    (give,) = normed_rows(True, carried, maps_conv, shown, passed, gain, (), "give_rows")
    taken = core_swap(give)
    keep, own_left, other_left = normed_rows(
        False, carried, maps_conv, shown, passed, gain, weights, "keep_rows"
    )
    columns = own_left.shape[1]
    far_a, up_a, down_a, own_a = project(keep, taken, own_left, other_left, columns, "left_half")
    far_b, up_b, down_b, own_b = project(
        keep, taken, out_weight, other_weight, columns, "right_half"
    )

    def added(*values):
        return functools.reduce(lambda a, b: a + b, [v.astype(F32) for v in values]).astype(BF16)

    relay_a = along(far_a, 1)
    from_above_a = along(down_a, -1)
    relay_b = along(far_b, -1)
    from_below_b = along(up_b, 1)
    from_below_a = along(added(up_a, relay_a), 1)
    from_above_b = along(added(down_b, relay_b), -1)
    return jnp.concatenate(
        [added(own_a, from_above_a, from_below_a), added(own_b, from_above_b, from_below_b)], axis=1
    )


def solution(mesh):
    return jax.shard_map(
        on_device,
        mesh=mesh,
        in_specs=(
            P("ctx", "tp"),
            P("ctx", "tp"),
            P("ctx", "tp"),
            P("ctx", "tp"),
            P("tp"),
            P("tp"),
            P("tp"),
            P(None, "tp"),
            P(None, "tp"),
            P("tp"),
            P("tp", None),
        ),
        out_specs=P(("ctx", "tp"), None),
        check_vma=False,
    )
```

```python
import functools

import jax
import jax.numpy as jnp
from jax import lax
from jax.experimental import pallas as pl
from jax.experimental.pallas import tpu as pltpu
from jax.sharding import PartitionSpec as P

BF16 = jnp.bfloat16
F32 = jnp.float32
VMEM_LIMIT = 16 * 1024 * 1024
TURNS = (2, 1, 3, 0)


def far_memory(value):
    return pltpu.with_memory_space_constraint(value, pltpu.HBM)


def params(**more):
    return pltpu.CompilerParams(vmem_limit_bytes=VMEM_LIMIT, **more)


def shifted(value, axis, steps):
    count = lax.axis_size(axis)
    leading, last = (max(0, -steps), min(count, count - steps))
    return lax.ppermute(value, axis, [(source, source + steps) for source in range(leading, last)])


def three_parts(value):
    high = value.astype(BF16)
    rest = value - high.astype(F32)
    middle = rest.astype(BF16)
    low = (rest - middle.astype(F32)).astype(BF16)
    return high, middle, low


def packed_parts(value):
    high, middle, low = three_parts(value)
    wide = [high.astype(F32), middle.astype(F32), low.astype(F32)]
    return jnp.concatenate(wide, axis=0).astype(BF16)


def head_selector(first_head, heads, head_dim, width):
    rows = lax.broadcasted_iota(jnp.int32, (3 * heads, width), 0)
    lanes = lax.broadcasted_iota(jnp.int32, (3 * heads, width), 1)
    return (rows % heads == first_head + lanes // head_dim).astype(F32).astype(BF16)


def spread_heads(parts, selector):
    return lax.dot_general(
        parts, selector, (((0,), (0,)), ((), ())), preferred_element_type=F32
    )


def silu(value):
    return value / (1.0 + jnp.exp(-value))


def conv_rows(padded, taps, start, rows):
    count = taps.shape[0]
    columns = []
    for column in range(taps.shape[1] // 128):
        total = None
        for offset in range(count):
            first = 8 - (count - 1) + offset + start
            weight = taps[offset : offset + 1, 128 * column : 128 * column + 128]
            term = weight * padded[column, pl.ds(first, rows), :]
            total = term if total is None else total + term
        columns.append(total)
    return columns[0] if len(columns) == 1 else jnp.concatenate(columns, axis=1)


def state_kernel(
    heads,
    head_dim,
    held,
    x_ref,
    x_taps_ref,
    maps_ref,
    maps_taps_ref,
    raw_ref,
    bias_ref,
    decay_ref,
    conv_ref,
    maps_conv_ref,
    step_ref,
    total_ref,
    first_tail_ref,
    reached_ref,
    padded,
    tail_parts,
    end_parts,
    weighted,
):
    column = pl.program_id(0)
    length, width = x_ref.shape
    tile = 128
    state = maps_ref.shape[1] // 2

    def fill(source):
        for column in range(source.shape[1] // 128):
            lanes = pl.ds(128 * column, 128)
            padded[column, pl.ds(0, 8), :] = jnp.zeros((8, 128), F32)
            for start in range(0, length, tile):
                rows = pl.ds(8 + start, tile)
                padded[column, rows, :] = source[pl.ds(start, tile), lanes].astype(F32)

    @pl.when(column == 0)
    def _():
        row_ids = lax.broadcasted_iota(jnp.int32, (heads, heads), 0)
        col_ids = lax.broadcasted_iota(jnp.int32, (heads, heads), 1)

        def as_column(ref):
            spread = jnp.where(row_ids == col_ids, ref[...], 0.0)
            return jnp.sum(spread, axis=1, keepdims=True)

        step = jnp.log1p(jnp.exp(raw_ref[...] + as_column(bias_ref)))
        step_ref[...] = step
        rate = step * jnp.exp(as_column(decay_ref))
        piece = 128
        source = lax.broadcasted_iota(jnp.int32, (piece, piece), 0)
        target = lax.broadcasted_iota(jnp.int32, (piece, piece), 1)
        triangle = (source <= target).astype(F32).astype(BF16)
        before = jnp.zeros((heads, 1), F32)
        for start in range(0, length, piece):
            parts = three_parts(rate[:, start : start + piece])
            sums = [jnp.dot(part, triangle, preferred_element_type=F32) for part in parts]
            block = sums[0] + (sums[1] + sums[2]) + before
            total_ref[:, pl.ds(start, piece)] = block
            before = block[:, piece - 1 : piece]
        tail_parts[...] = packed_parts(jnp.exp(total_ref[...] - before) * step)
        end_parts[...] = packed_parts(jnp.broadcast_to(jnp.exp(-before), (heads, 128)))
        first_tail_ref[...] = tail_parts[:, :128]
        fill(maps_ref)
        taps = maps_taps_ref[...].astype(F32)
        for start in range(0, length, tile):
            rows = silu(conv_rows(padded, taps, start, tile))
            maps_conv_ref[pl.ds(start, tile), :] = rows.astype(BF16)

    fill(x_ref)
    taps = x_taps_ref[...].astype(F32)
    selector = head_selector(column * (width // head_dim), heads, head_dim, width)
    for start in range(0, length, tile):
        rows = silu(conv_rows(padded, taps, start, tile)).astype(BF16)
        conv_ref[pl.ds(start, tile), :] = rows
        tail = spread_heads(tail_parts[:, start : start + tile], selector)
        scaled = tail * rows.astype(F32)
        if start == 0:
            ids = lax.broadcasted_iota(jnp.int32, scaled.shape, 0)
            scaled = jnp.where(ids >= held, scaled, 0.0)
        weighted[pl.ds(start, tile), :] = scaled.astype(BF16)
    reached = lax.dot_general(
        maps_conv_ref[:, :state],
        weighted[...],
        (((0,), (0,)), ((), ())),
        preferred_element_type=F32,
    )
    factor = spread_heads(end_parts[:, :8], selector)
    high, middle, low = [part.astype(F32) for part in three_parts(factor)]
    ids = lax.broadcasted_iota(jnp.int32, factor.shape, 0)
    extra = jnp.where(ids == 0, high, jnp.where(ids == 1, middle, jnp.where(ids == 2, low, 0.0)))
    per_column = reached_ref.shape[0] // (width // 128)
    depth = state // per_column
    for piece in range(reached_ref.shape[0]):
        lanes = slice(128 * (piece // per_column), 128 * (piece // per_column) + 128)
        first = depth * (piece % per_column)
        reached_ref[piece, pl.ds(0, depth), :] = reached[first : first + depth, lanes]
        reached_ref[piece, pl.ds(depth, 8), :] = extra[:, lanes]


def local_states(x, x_taps, maps, maps_taps, raw, bias, decay_log, blocks, held):
    length, channels = x.shape
    heads = raw.shape[0]
    maps_width = maps.shape[1]
    width = 512
    columns = channels // width
    taps = x_taps.shape[0]
    state = maps_width // 2
    reached = (blocks, state * channels // (blocks * 128) + 8, 128)
    whole = lambda shape: pl.BlockSpec(shape, lambda i: (0,) * len(shape))
    return pl.pallas_call(
        functools.partial(state_kernel, heads, channels // heads, held),
        grid=(columns,),
        in_specs=[
            pl.BlockSpec((length, width), lambda i: (0, i)),
            pl.BlockSpec((taps, width), lambda i: (0, i)),
            whole((length, maps_width)),
            whole((taps, maps_width)),
            whole((heads, length)),
            whole((1, heads)),
            whole((1, heads)),
        ],
        out_specs=[
            pl.BlockSpec((length, width), lambda i: (0, i)),
            whole((length, maps_width)),
            whole((heads, length)),
            whole((heads, length)),
            whole((3 * heads, 128)),
            pl.BlockSpec((blocks // columns,) + reached[1:], lambda i: (i, 0, 0)),
        ],
        out_shape=[
            pltpu.HBM((length, channels), BF16),
            jax.ShapeDtypeStruct((length, maps_width), BF16),
            jax.ShapeDtypeStruct((heads, length), F32),
            jax.ShapeDtypeStruct((heads, length), F32),
            jax.ShapeDtypeStruct((3 * heads, 128), BF16),
            jax.ShapeDtypeStruct(reached, F32),
        ],
        scratch_shapes=[
            pltpu.VMEM((width // 128, length + 8, 128), F32),
            pltpu.VMEM((3 * heads, length), BF16),
            pltpu.VMEM((3 * heads, 128), BF16),
            pltpu.VMEM((length, width), BF16),
        ],
        compiler_params=params(),
        cost_estimate=pl.CostEstimate(
            flops=5_000_000_000, bytes_accessed=4_000_000, transcendentals=0
        ),
        name="local_states",
    )(x, x_taps, maps, maps_taps, raw, bias, decay_log)


def first_rows_kernel(
    head_dim,
    x_ref,
    maps_ref,
    halo_ref,
    x_taps_ref,
    maps_taps_ref,
    first_tail_ref,
    reached_ref,
    conv_in_ref,
    maps_conv_in_ref,
    conv_ref,
    maps_conv_ref,
    sent_ref,
    padded,
):
    held, channels = x_ref.shape
    maps_width = maps_ref.shape[1]
    leading = halo_ref.shape[0]
    state = maps_width // 2
    heads = first_tail_ref.shape[0] // 3
    for column in range(padded.shape[0]):
        lanes = pl.ds(128 * column, 128)
        padded[column, pl.ds(8 - leading, leading), :] = halo_ref[:, lanes].astype(F32)
        source, first = (x_ref, 0) if 128 * column < channels else (maps_ref, channels)
        lanes = pl.ds(128 * column - first, 128)
        padded[column, pl.ds(8, held), :] = source[:, lanes].astype(F32)
    taps = jnp.concatenate([x_taps_ref[...].astype(F32), maps_taps_ref[...].astype(F32)], axis=1)
    rows = silu(conv_rows(padded, taps, 0, held)).astype(BF16)
    conv_ref[...] = rows[:, :channels]
    maps_conv_ref[...] = rows[:, channels:]
    selector = head_selector(0, heads, head_dim, channels)
    tail = spread_heads(first_tail_ref[:, :held], selector)
    weighted = (tail * rows[:, :channels].astype(F32)).astype(BF16)
    more = lax.dot_general(
        rows[:, channels : channels + state],
        weighted,
        (((0,), (0,)), ((), ())),
        preferred_element_type=F32,
    )
    pieces = sent_ref.shape[0]
    per_column = pieces // (channels // 128)
    depth = state // per_column
    for piece in range(pieces):
        lanes = slice(128 * (piece // per_column), 128 * (piece // per_column) + 128)
        first = depth * (piece % per_column)
        sent_ref[piece] = jnp.concatenate(
            [
                reached_ref[piece, pl.ds(0, depth), :] + more[first : first + depth, lanes],
                reached_ref[piece, pl.ds(depth, 8), :],
            ],
            axis=0,
        ).astype(BF16)


def first_rows(x, maps, halo, x_taps, maps_taps, first_tail, reached, conv, maps_conv, held):
    heads = first_tail.shape[0] // 3
    channels, maps_width = x.shape[1], maps.shape[1]
    whole = lambda array: pl.BlockSpec(array.shape, lambda i: (0,) * array.ndim)
    head = lambda array: pl.BlockSpec((held, array.shape[1]), lambda i: (0, 0))
    near = pl.BlockSpec(memory_space=pltpu.VMEM)
    return pl.pallas_call(
        functools.partial(first_rows_kernel, channels // heads),
        grid=(1,),
        in_specs=[
            head(x),
            head(maps),
            near,
            whole(x_taps),
            whole(maps_taps),
            near,
            near,
            pl.BlockSpec(memory_space=pl.ANY),
            pl.BlockSpec(memory_space=pl.ANY),
        ],
        out_specs=[head(conv), head(maps_conv), whole(reached)],
        out_shape=[
            pltpu.HBM(conv.shape, BF16),
            jax.ShapeDtypeStruct(maps_conv.shape, BF16),
            jax.ShapeDtypeStruct(reached.shape, BF16),
        ],
        scratch_shapes=[pltpu.VMEM(((channels + maps_width) // 128, held + 8, 128), F32)],
        input_output_aliases={7: 0, 8: 1},
        compiler_params=params(),
        name="first_rows",
    )(x, maps, halo, x_taps, maps_taps, first_tail, reached, conv, maps_conv)


def scan_kernel(got_ref, out_ref):
    blocks, rows, lanes = out_ref.shape
    running = jnp.zeros((rows, lanes), F32)
    for block in range(blocks):
        out_ref[block] = running.astype(BF16)
        if block < blocks - 1:
            piece = got_ref[block].astype(F32)
            factor = piece[rows : rows + 1] + (
                piece[rows + 1 : rows + 2] + piece[rows + 2 : rows + 3]
            )
            running = factor * running + piece[:rows]


def scan_blocks(got):
    blocks, rows, lanes = got.shape
    return pl.pallas_call(
        scan_kernel,
        out_shape=jax.ShapeDtypeStruct((blocks, rows - 8, lanes), BF16),
        compiler_params=params(),
        name="scan_blocks",
    )(got)


def local_kernel(
    head_dim, x_ref, maps_ref, z_ref, step_ref, total_ref, skip_ref, shown_ref, passed_ref, scores
):
    pair = pl.program_id(0)
    length, width = x_ref.shape
    state = maps_ref.shape[1] // 2
    per_step = width // head_dim
    tile = 128

    @pl.when(pair == 0)
    def _():
        scores[...] = lax.dot_general(
            maps_ref[:, state:],
            maps_ref[:, :state],
            (((1,), (1,)), ((), ())),
            preferred_element_type=F32,
        )

    later = lax.broadcasted_iota(jnp.int32, (tile, tile), 0)
    earlier = lax.broadcasted_iota(jnp.int32, (tile, tile), 1)
    causal = later >= earlier
    lanes = lax.broadcasted_iota(jnp.int32, (tile, width), 1)
    totals = [total_ref[pl.ds(pair * per_step + head, 1), :] for head in range(per_step)]
    steps = [step_ref[pl.ds(pair * per_step + head, 1), :] for head in range(per_step)]
    skip = skip_ref[pair * per_step]
    for head in range(1, per_step):
        skip = jnp.where(lanes >= head * head_dim, skip_ref[pair * per_step + head], skip)
    for start in range(0, length, tile):
        outs = []
        outer = None
        for head in range(per_step):
            columns = jnp.broadcast_to(totals[head][:, start : start + tile], (tile, tile)).T
            weights = []
            for source in range(0, start + tile, tile):
                spread = totals[head][:, source : source + tile] - columns
                if source == start:
                    spread = jnp.where(causal, spread, -1e30)
                part = jnp.exp(spread) * scores[pl.ds(start, tile), pl.ds(source, tile)]
                part = part * steps[head][:, source : source + tile]
                weights.append(part.astype(BF16))
            weights = weights[0] if len(weights) == 1 else jnp.concatenate(weights, axis=1)
            outs.append(
                jnp.dot(
                    weights,
                    x_ref[pl.ds(0, start + tile), pl.ds(head * head_dim, head_dim)],
                    preferred_element_type=F32,
                )
            )
            fade = jnp.exp(-columns)
            outer = fade if outer is None else jnp.where(lanes >= head * head_dim, fade, outer)
        values = x_ref[pl.ds(start, tile), :].astype(F32)
        gate = silu(z_ref[pl.ds(start, tile), :].astype(F32))
        out = jnp.concatenate(outs, axis=1) + skip * values
        shown_ref[pl.ds(start, tile), :] = (out * gate).astype(BF16)
        passed_ref[pl.ds(start, tile), :] = (outer * gate).astype(BF16)


def local_outputs(x_conv, maps_conv, z, step_rows, total_rows, skip, head_dim):
    length, channels = x_conv.shape
    width = 128
    columns = channels // width
    heads = channels // head_dim
    maps_width = maps_conv.shape[1]
    block = pl.BlockSpec((length, width), lambda i: (0, i))
    row_block = pl.BlockSpec((heads, length), lambda i: (0, 0))
    return pl.pallas_call(
        functools.partial(local_kernel, head_dim),
        grid=(columns,),
        in_specs=[
            block,
            pl.BlockSpec((length, maps_width), lambda i: (0, 0)),
            block,
            row_block,
            row_block,
            pl.BlockSpec(memory_space=pltpu.SMEM),
        ],
        out_specs=[block, block],
        out_shape=[jax.ShapeDtypeStruct((length, channels), BF16)] * 2,
        scratch_shapes=[pltpu.VMEM((length, length), F32)],
        compiler_params=params(),
        cost_estimate=pl.CostEstimate(
            flops=8_000_000_000, bytes_accessed=6_000_000, transcendentals=0
        ),
        name="local_outputs",
    )(x_conv, maps_conv, z, step_rows, total_rows, skip)


def fetches(sources, targets, columns, arrived):
    pieces = 4
    copies = []
    for index, (source, target) in enumerate(zip(sources, targets)):
        depth = target.shape[0] // pieces
        for piece in range(pieces):
            rows = pl.ds(piece * depth, depth)
            copies.append(
                pltpu.make_async_copy(
                    source.at[rows, columns],
                    target.at[rows, :],
                    arrived.at[index * pieces + piece],
                )
            )
    return copies


def norm_kernel(other, carried_ref, maps_ref, shown_ref, passed_ref, gain_ref, *rest):
    copies = []
    if other:
        out_ref, entering = rest
    else:
        sources, out_ref, targets, (entering, arrived) = rest[:2], rest[2], rest[3:5], rest[5:]
        copies = fetches(sources, targets, pl.ds(0, targets[0].shape[1]), arrived)
    for copy in copies:
        copy.start()
    state, channels = entering.shape
    pieces, depth, lanes = carried_ref.shape
    per_column = state // depth
    for piece in range(pieces):
        entering[
            pl.ds(depth * (piece % per_column), depth),
            pl.ds(lanes * (piece // per_column), lanes),
        ] = carried_ref[piece]
    ring = len(TURNS)
    size = out_ref.shape[0] // ring
    place = lax.axis_index("tp")
    across, core = place // 2, lax.rem(place, 2)
    if other:
        core = 1 - core
    for turn, ahead in enumerate(TURNS):
        pick = 2 * lax.rem(across + ahead, ring) + core
        rows = pl.ds(pl.multiple_of(pick * size, size), size)
        carry = jnp.dot(maps_ref[rows, state:], entering[...], preferred_element_type=F32)
        gated = shown_ref[rows, :].astype(F32) + carry * passed_ref[rows, :].astype(F32)
        scale = lax.rsqrt(jnp.mean(gated * gated, axis=1, keepdims=True) + 1e-05)
        out_ref[pl.ds(size * turn, size), :] = (gated * scale * gain_ref[...]).astype(BF16)
    for copy in copies:
        copy.wait()


def normed_rows(other, carried, maps_conv, shown, passed, gain, weights, name):
    length, channels = shown.shape
    state = maps_conv.shape[1] // 2
    near = pl.BlockSpec(memory_space=pltpu.VMEM)
    far = pl.BlockSpec(memory_space=pltpu.HBM)
    normed = jax.ShapeDtypeStruct((length // 2, channels), BF16)
    scratch = [pltpu.VMEM((state, channels), BF16)]
    fetched = []
    if not other:
        fetched = [jax.ShapeDtypeStruct((w.shape[0], w.shape[1] // 2), BF16) for w in weights]
        scratch.append(pltpu.SemaphoreType.DMA((8,)))
    return pl.pallas_call(
        functools.partial(norm_kernel, other),
        in_specs=[near] * 5 + [far] * len(weights),
        out_specs=[near] * (1 + len(fetched)),
        scratch_shapes=scratch,
        out_shape=[normed] + fetched,
        compiler_params=params(),
        cost_estimate=pl.CostEstimate(
            flops=1_000_000_000, bytes_accessed=3_000_000, transcendentals=0
        ),
        name=name,
    )(carried, maps_conv, shown, passed, gain, *[far_memory(weight) for weight in weights])


def project_near_kernel(own_ref, other_ref, own_weight_ref, other_weight_ref, *out_refs):
    rows, columns = out_refs[0].shape
    width = 512
    for start in range(0, columns, width):
        lanes = pl.ds(start, width)
        product = jnp.dot(own_ref[...], own_weight_ref[:, lanes], preferred_element_type=F32)
        product = product + jnp.dot(
            other_ref[...], other_weight_ref[:, lanes], preferred_element_type=F32
        )
        for index, out_ref in enumerate(out_refs):
            piece = product[rows * index : rows * (index + 1)]
            out_ref[:, lanes] = piece.astype(out_ref.dtype)


def project_far_kernel(own_ref, other_ref, own_weight_ref, other_weight_ref, *rest):
    out_refs, (own_near, other_near, total, arrived) = rest[:4], rest[4:]
    rows, columns = out_refs[0].shape
    width = 512
    copies = fetches(
        (own_weight_ref, other_weight_ref),
        (own_near, other_near),
        pl.ds(columns, columns),
        arrived,
    )
    half = len(copies) // 2
    for copy in copies:
        copy.start()
    for copy in copies[:half]:
        copy.wait()
    for start in range(0, columns, width):
        lanes = pl.ds(start, width)
        total[:, lanes] = jnp.dot(
            own_ref[...], own_near[:, lanes], preferred_element_type=F32
        )
    for copy in copies[half:]:
        copy.wait()
    for start in range(0, columns, width):
        lanes = pl.ds(start, width)
        product = total[:, lanes] + jnp.dot(
            other_ref[...], other_near[:, lanes], preferred_element_type=F32
        )
        for index, out_ref in enumerate(out_refs):
            piece = product[rows * index : rows * (index + 1)]
            out_ref[:, lanes] = piece.astype(out_ref.dtype)


def project(own, other, own_weight, other_weight, columns, name):
    count, depth = own.shape
    near = pl.BlockSpec(memory_space=pltpu.VMEM)
    far = own_weight.shape[1] > columns
    weight_spec = pl.BlockSpec(memory_space=pltpu.HBM) if far else near
    weights = [own_weight, other_weight]
    return pl.pallas_call(
        project_far_kernel if far else project_near_kernel,
        in_specs=[near, near, weight_spec, weight_spec],
        out_specs=[near] * 4,
        out_shape=[jax.ShapeDtypeStruct((count // 4, columns), BF16)] * 4,
        scratch_shapes=[
            pltpu.VMEM((depth, columns), BF16),
            pltpu.VMEM((depth, columns), BF16),
            pltpu.VMEM((count, columns), F32),
            pltpu.SemaphoreType.DMA((8,)),
        ]
        if far
        else [],
        compiler_params=params(),
        cost_estimate=pl.CostEstimate(
            flops=4 * count * depth * columns, bytes_accessed=9_000_000, transcendentals=0
        ),
        name=name,
    )(own, other, *([far_memory(weight) for weight in weights] if far else weights))


def last_rows_kernel(x_ref, maps_ref, out_ref):
    count = out_ref.shape[0]
    channels = x_ref.shape[1]
    first = x_ref.shape[0] - count
    out_ref[:, :channels] = x_ref[...].astype(F32)[first:].astype(BF16)
    out_ref[:, channels:] = maps_ref[...].astype(F32)[first:].astype(BF16)


def last_rows(x, maps, count, held):
    last = x.shape[0] // held - 1
    tail = lambda array: pl.BlockSpec((held, array.shape[1]), lambda i: (last, 0))
    shape = (count, x.shape[1] + maps.shape[1])
    return pl.pallas_call(
        last_rows_kernel,
        grid=(1,),
        in_specs=[tail(x), tail(maps)],
        out_specs=pl.BlockSpec(memory_space=pltpu.VMEM),
        out_shape=jax.ShapeDtypeStruct(shape, BF16),
        compiler_params=params(),
        name="last_rows",
    )(x, maps)


def on_device(
    x_inputs,
    state_maps,
    z_gate,
    step_raw,
    step_bias,
    decay_log,
    skip_gain,
    x_filter,
    state_filter,
    norm_gain,
    out_weight,
):
    length, channels = x_inputs.shape
    leading = x_filter.shape[0] - 1
    heads = step_raw.shape[1]
    head_dim = channels // heads
    blocks = lax.axis_size("ctx")
    members = lax.axis_size("tp")
    ring = members // 2

    def core_swap(value):
        return lax.ppermute(value, "tp", [(i, i ^ 1) for i in range(members)])

    def along(value, steps):
        pairs = [
            (2 * y + c, 2 * ((y + steps) % ring) + c) for y in range(ring) for c in range(2)
        ]
        return lax.ppermute(value, "tp", pairs)

    held = 16
    x_inputs, state_maps = far_memory(x_inputs), far_memory(state_maps)
    halo = shifted(last_rows(x_inputs, state_maps, leading, held), "ctx", 1)
    x_filter, state_filter = far_memory(x_filter), far_memory(state_filter)
    conv, maps_conv, step, total, first_tail, reached = local_states(
        x_inputs,
        x_filter,
        state_maps,
        state_filter,
        far_memory(step_raw.T),
        far_memory(step_bias[None]),
        far_memory(decay_log[None]),
        blocks,
        held,
    )
    other_weight = core_swap(lax.optimization_barrier((out_weight, halo, first_tail))[0])
    x_conv, maps_conv, sent = first_rows(
        x_inputs,
        state_maps,
        halo,
        x_filter,
        state_filter,
        first_tail,
        reached,
        conv,
        maps_conv,
        held,
    )
    got = lax.all_to_all(sent, "ctx", 0, 0, tiled=True)
    shown, passed = local_outputs(
        x_conv,
        maps_conv,
        far_memory(z_gate),
        step,
        total,
        skip_gain,
        head_dim,
    )
    got, shown, passed = lax.optimization_barrier((got, shown, passed))
    entering = scan_blocks(got)
    carried = lax.all_to_all(entering, "ctx", 0, 0, tiled=True)

    gain = norm_gain[None]
    weights = (out_weight, other_weight)
    (give,) = normed_rows(True, carried, maps_conv, shown, passed, gain, (), "give_rows")
    taken = core_swap(give)
    keep, own_left, other_left = normed_rows(
        False, carried, maps_conv, shown, passed, gain, weights, "keep_rows"
    )
    columns = own_left.shape[1]
    far_a, up_a, down_a, own_a = project(keep, taken, own_left, other_left, columns, "left_half")
    far_b, up_b, down_b, own_b = project(
        keep, taken, out_weight, other_weight, columns, "right_half"
    )

    def added(*values):
        return functools.reduce(lambda a, b: a + b, [v.astype(F32) for v in values]).astype(BF16)

    relay_a = along(far_a, 1)
    from_above_a = along(down_a, -1)
    relay_b = along(far_b, -1)
    from_below_b = along(up_b, 1)
    from_below_a = along(added(up_a, relay_a), 1)
    from_above_b = along(added(down_b, relay_b), -1)
    return jnp.concatenate(
        [added(own_a, from_above_a, from_below_a), added(own_b, from_above_b, from_below_b)], axis=1
    )


def solution(mesh):
    return jax.shard_map(
        on_device,
        mesh=mesh,
        in_specs=(
            P("ctx", "tp"),
            P("ctx", "tp"),
            P("ctx", "tp"),
            P("ctx", "tp"),
            P("tp"),
            P("tp"),
            P("tp"),
            P(None, "tp"),
            P(None, "tp"),
            P("tp"),
            P("tp", None),
        ),
        out_specs=P(("ctx", "tp"), None),
        check_vma=False,
    )
```

```python
import functools

import jax
import jax.numpy as jnp
from jax import lax
from jax.experimental import pallas as pl
from jax.experimental.pallas import tpu as pltpu
from jax.sharding import PartitionSpec as P

BF16 = jnp.bfloat16
F32 = jnp.float32
VMEM_LIMIT = 16 * 1024 * 1024
TURNS = (2, 1, 3, 0)


def far_memory(value):
    return pltpu.with_memory_space_constraint(value, pltpu.HBM)


def params(**more):
    return pltpu.CompilerParams(vmem_limit_bytes=VMEM_LIMIT, **more)


def shifted(value, axis, steps):
    count = lax.axis_size(axis)
    leading, last = (max(0, -steps), min(count, count - steps))
    return lax.ppermute(value, axis, [(source, source + steps) for source in range(leading, last)])


def three_parts(value):
    high = value.astype(BF16)
    rest = value - high.astype(F32)
    middle = rest.astype(BF16)
    low = (rest - middle.astype(F32)).astype(BF16)
    return high, middle, low


def packed_parts(value):
    high, middle, low = three_parts(value)
    wide = [high.astype(F32), middle.astype(F32), low.astype(F32)]
    return jnp.concatenate(wide, axis=0).astype(BF16)


def head_selector(first_head, heads, head_dim, width):
    rows = lax.broadcasted_iota(jnp.int32, (3 * heads, width), 0)
    lanes = lax.broadcasted_iota(jnp.int32, (3 * heads, width), 1)
    return (rows % heads == first_head + lanes // head_dim).astype(F32).astype(BF16)


def spread_heads(parts, selector):
    return lax.dot_general(
        parts, selector, (((0,), (0,)), ((), ())), preferred_element_type=F32
    )


def silu(value):
    return value / (1.0 + jnp.exp(-value))


def conv_rows(padded, taps, start, rows):
    count = taps.shape[0]
    columns = []
    for column in range(taps.shape[1] // 128):
        total = None
        for offset in range(count):
            first = 8 - (count - 1) + offset + start
            weight = taps[offset : offset + 1, 128 * column : 128 * column + 128]
            term = weight * padded[column, pl.ds(first, rows), :]
            total = term if total is None else total + term
        columns.append(total)
    return columns[0] if len(columns) == 1 else jnp.concatenate(columns, axis=1)


def state_kernel(
    heads,
    head_dim,
    held,
    x_ref,
    x_taps_ref,
    maps_ref,
    maps_taps_ref,
    raw_ref,
    bias_ref,
    decay_ref,
    conv_ref,
    maps_conv_ref,
    step_ref,
    total_ref,
    first_tail_ref,
    reached_ref,
    padded,
    tail_parts,
    end_parts,
    weighted,
):
    column = pl.program_id(0)
    length, width = x_ref.shape
    tile = 128
    state = maps_ref.shape[1] // 2

    def fill(source):
        for column in range(source.shape[1] // 128):
            lanes = pl.ds(128 * column, 128)
            padded[column, pl.ds(0, 8), :] = jnp.zeros((8, 128), F32)
            for start in range(0, length, tile):
                rows = pl.ds(8 + start, tile)
                padded[column, rows, :] = source[pl.ds(start, tile), lanes].astype(F32)

    @pl.when(column == 0)
    def _():
        row_ids = lax.broadcasted_iota(jnp.int32, (heads, heads), 0)
        col_ids = lax.broadcasted_iota(jnp.int32, (heads, heads), 1)

        def as_column(ref):
            spread = jnp.where(row_ids == col_ids, ref[...], 0.0)
            return jnp.sum(spread, axis=1, keepdims=True)

        step = jnp.log1p(jnp.exp(raw_ref[...] + as_column(bias_ref)))
        step_ref[...] = step
        rate = step * jnp.exp(as_column(decay_ref))
        piece = 128
        source = lax.broadcasted_iota(jnp.int32, (piece, piece), 0)
        target = lax.broadcasted_iota(jnp.int32, (piece, piece), 1)
        triangle = (source <= target).astype(F32).astype(BF16)
        before = jnp.zeros((heads, 1), F32)
        for start in range(0, length, piece):
            parts = three_parts(rate[:, start : start + piece])
            sums = [jnp.dot(part, triangle, preferred_element_type=F32) for part in parts]
            block = sums[0] + (sums[1] + sums[2]) + before
            total_ref[:, pl.ds(start, piece)] = block
            before = block[:, piece - 1 : piece]
        tail_parts[...] = packed_parts(jnp.exp(total_ref[...] - before) * step)
        end_parts[...] = packed_parts(jnp.broadcast_to(jnp.exp(-before), (heads, 128)))
        first_tail_ref[...] = tail_parts[:, :128]
        fill(maps_ref)
        taps = maps_taps_ref[...].astype(F32)
        for start in range(0, length, tile):
            rows = silu(conv_rows(padded, taps, start, tile))
            maps_conv_ref[pl.ds(start, tile), :] = rows.astype(BF16)

    fill(x_ref)
    taps = x_taps_ref[...].astype(F32)
    selector = head_selector(column * (width // head_dim), heads, head_dim, width)
    for start in range(0, length, tile):
        rows = silu(conv_rows(padded, taps, start, tile)).astype(BF16)
        conv_ref[pl.ds(start, tile), :] = rows
        tail = spread_heads(tail_parts[:, start : start + tile], selector)
        scaled = tail * rows.astype(F32)
        if start == 0:
            ids = lax.broadcasted_iota(jnp.int32, scaled.shape, 0)
            scaled = jnp.where(ids >= held, scaled, 0.0)
        weighted[pl.ds(start, tile), :] = scaled.astype(BF16)
    reached = lax.dot_general(
        maps_conv_ref[:, :state],
        weighted[...],
        (((0,), (0,)), ((), ())),
        preferred_element_type=F32,
    )
    factor = spread_heads(end_parts[:, :8], selector)
    high, middle, low = [part.astype(F32) for part in three_parts(factor)]
    ids = lax.broadcasted_iota(jnp.int32, factor.shape, 0)
    extra = jnp.where(ids == 0, high, jnp.where(ids == 1, middle, jnp.where(ids == 2, low, 0.0)))
    per_column = reached_ref.shape[0] // (width // 128)
    depth = state // per_column
    for piece in range(reached_ref.shape[0]):
        lanes = slice(128 * (piece // per_column), 128 * (piece // per_column) + 128)
        first = depth * (piece % per_column)
        reached_ref[piece, pl.ds(0, depth), :] = reached[first : first + depth, lanes]
        reached_ref[piece, pl.ds(depth, 8), :] = extra[:, lanes]


def local_states(x, x_taps, maps, maps_taps, raw, bias, decay_log, blocks, held):
    length, channels = x.shape
    heads = raw.shape[0]
    maps_width = maps.shape[1]
    width = 512
    columns = channels // width
    taps = x_taps.shape[0]
    state = maps_width // 2
    reached = (blocks, state * channels // (blocks * 128) + 8, 128)
    whole = lambda shape: pl.BlockSpec(shape, lambda i: (0,) * len(shape))
    return pl.pallas_call(
        functools.partial(state_kernel, heads, channels // heads, held),
        grid=(columns,),
        in_specs=[
            pl.BlockSpec((length, width), lambda i: (0, i)),
            pl.BlockSpec((taps, width), lambda i: (0, i)),
            whole((length, maps_width)),
            whole((taps, maps_width)),
            whole((heads, length)),
            whole((1, heads)),
            whole((1, heads)),
        ],
        out_specs=[
            pl.BlockSpec((length, width), lambda i: (0, i)),
            whole((length, maps_width)),
            whole((heads, length)),
            whole((heads, length)),
            whole((3 * heads, 128)),
            pl.BlockSpec((blocks // columns,) + reached[1:], lambda i: (i, 0, 0)),
        ],
        out_shape=[
            pltpu.HBM((length, channels), BF16),
            jax.ShapeDtypeStruct((length, maps_width), BF16),
            jax.ShapeDtypeStruct((heads, length), F32),
            jax.ShapeDtypeStruct((heads, length), F32),
            jax.ShapeDtypeStruct((3 * heads, 128), BF16),
            jax.ShapeDtypeStruct(reached, F32),
        ],
        scratch_shapes=[
            pltpu.VMEM((width // 128, length + 8, 128), F32),
            pltpu.VMEM((3 * heads, length), BF16),
            pltpu.VMEM((3 * heads, 128), BF16),
            pltpu.VMEM((length, width), BF16),
        ],
        compiler_params=params(),
        cost_estimate=pl.CostEstimate(
            flops=5_000_000_000, bytes_accessed=4_000_000, transcendentals=0
        ),
        name="local_states",
    )(x, x_taps, maps, maps_taps, raw, bias, decay_log)


def first_rows_kernel(
    head_dim,
    x_ref,
    maps_ref,
    halo_ref,
    x_taps_ref,
    maps_taps_ref,
    first_tail_ref,
    reached_ref,
    conv_in_ref,
    maps_conv_in_ref,
    conv_ref,
    maps_conv_ref,
    sent_ref,
    padded,
):
    held, channels = x_ref.shape
    maps_width = maps_ref.shape[1]
    leading = halo_ref.shape[0]
    state = maps_width // 2
    heads = first_tail_ref.shape[0] // 3
    for column in range(padded.shape[0]):
        lanes = pl.ds(128 * column, 128)
        padded[column, pl.ds(8 - leading, leading), :] = halo_ref[:, lanes].astype(F32)
        source, first = (x_ref, 0) if 128 * column < channels else (maps_ref, channels)
        lanes = pl.ds(128 * column - first, 128)
        padded[column, pl.ds(8, held), :] = source[:, lanes].astype(F32)
    taps = jnp.concatenate([x_taps_ref[...].astype(F32), maps_taps_ref[...].astype(F32)], axis=1)
    rows = silu(conv_rows(padded, taps, 0, held)).astype(BF16)
    conv_ref[...] = rows[:, :channels]
    maps_conv_ref[...] = rows[:, channels:]
    selector = head_selector(0, heads, head_dim, channels)
    tail = spread_heads(first_tail_ref[:, :held], selector)
    weighted = (tail * rows[:, :channels].astype(F32)).astype(BF16)
    more = lax.dot_general(
        rows[:, channels : channels + state],
        weighted,
        (((0,), (0,)), ((), ())),
        preferred_element_type=F32,
    )
    pieces = sent_ref.shape[0]
    per_column = pieces // (channels // 128)
    depth = state // per_column
    for piece in range(pieces):
        lanes = slice(128 * (piece // per_column), 128 * (piece // per_column) + 128)
        first = depth * (piece % per_column)
        sent_ref[piece] = jnp.concatenate(
            [
                reached_ref[piece, pl.ds(0, depth), :] + more[first : first + depth, lanes],
                reached_ref[piece, pl.ds(depth, 8), :],
            ],
            axis=0,
        ).astype(BF16)


def first_rows(x, maps, halo, x_taps, maps_taps, first_tail, reached, conv, maps_conv, held):
    heads = first_tail.shape[0] // 3
    channels, maps_width = x.shape[1], maps.shape[1]
    whole = lambda array: pl.BlockSpec(array.shape, lambda i: (0,) * array.ndim)
    head = lambda array: pl.BlockSpec((held, array.shape[1]), lambda i: (0, 0))
    near = pl.BlockSpec(memory_space=pltpu.VMEM)
    return pl.pallas_call(
        functools.partial(first_rows_kernel, channels // heads),
        grid=(1,),
        in_specs=[
            head(x),
            head(maps),
            near,
            whole(x_taps),
            whole(maps_taps),
            near,
            near,
            pl.BlockSpec(memory_space=pl.ANY),
            pl.BlockSpec(memory_space=pl.ANY),
        ],
        out_specs=[head(conv), head(maps_conv), whole(reached)],
        out_shape=[
            pltpu.HBM(conv.shape, BF16),
            jax.ShapeDtypeStruct(maps_conv.shape, BF16),
            jax.ShapeDtypeStruct(reached.shape, BF16),
        ],
        scratch_shapes=[pltpu.VMEM(((channels + maps_width) // 128, held + 8, 128), F32)],
        input_output_aliases={7: 0, 8: 1},
        compiler_params=params(),
        name="first_rows",
    )(x, maps, halo, x_taps, maps_taps, first_tail, reached, conv, maps_conv)


def scan_kernel(got_ref, out_ref):
    blocks, rows, lanes = out_ref.shape
    running = jnp.zeros((rows, lanes), F32)
    for block in range(blocks):
        out_ref[block] = running.astype(BF16)
        if block < blocks - 1:
            piece = got_ref[block].astype(F32)
            factor = piece[rows : rows + 1] + (
                piece[rows + 1 : rows + 2] + piece[rows + 2 : rows + 3]
            )
            running = factor * running + piece[:rows]


def scan_blocks(got):
    blocks, rows, lanes = got.shape
    return pl.pallas_call(
        scan_kernel,
        out_shape=jax.ShapeDtypeStruct((blocks, rows - 8, lanes), BF16),
        compiler_params=params(),
        name="scan_blocks",
    )(got)


def local_kernel(
    head_dim, x_ref, maps_ref, z_ref, step_ref, total_ref, skip_ref, shown_ref, passed_ref, scores
):
    pair = pl.program_id(0)
    length, width = x_ref.shape
    state = maps_ref.shape[1] // 2
    per_step = width // head_dim
    tile = 128

    @pl.when(pair == 0)
    def _():
        scores[...] = lax.dot_general(
            maps_ref[:, state:],
            maps_ref[:, :state],
            (((1,), (1,)), ((), ())),
            preferred_element_type=F32,
        )

    later = lax.broadcasted_iota(jnp.int32, (tile, tile), 0)
    earlier = lax.broadcasted_iota(jnp.int32, (tile, tile), 1)
    causal = later >= earlier
    lanes = lax.broadcasted_iota(jnp.int32, (tile, width), 1)
    totals = [total_ref[pl.ds(pair * per_step + head, 1), :] for head in range(per_step)]
    steps = [step_ref[pl.ds(pair * per_step + head, 1), :] for head in range(per_step)]
    skip = skip_ref[pair * per_step]
    for head in range(1, per_step):
        skip = jnp.where(lanes >= head * head_dim, skip_ref[pair * per_step + head], skip)
    for start in range(0, length, tile):
        outs = []
        outer = None
        for head in range(per_step):
            columns = jnp.broadcast_to(totals[head][:, start : start + tile], (tile, tile)).T
            weights = []
            for source in range(0, start + tile, tile):
                spread = totals[head][:, source : source + tile] - columns
                if source == start:
                    spread = jnp.where(causal, spread, -1e30)
                part = jnp.exp(spread) * scores[pl.ds(start, tile), pl.ds(source, tile)]
                part = part * steps[head][:, source : source + tile]
                weights.append(part.astype(BF16))
            weights = weights[0] if len(weights) == 1 else jnp.concatenate(weights, axis=1)
            outs.append(
                jnp.dot(
                    weights,
                    x_ref[pl.ds(0, start + tile), pl.ds(head * head_dim, head_dim)],
                    preferred_element_type=F32,
                )
            )
            fade = jnp.exp(-columns)
            outer = fade if outer is None else jnp.where(lanes >= head * head_dim, fade, outer)
        values = x_ref[pl.ds(start, tile), :].astype(F32)
        gate = silu(z_ref[pl.ds(start, tile), :].astype(F32))
        out = jnp.concatenate(outs, axis=1) + skip * values
        shown_ref[pl.ds(start, tile), :] = (out * gate).astype(BF16)
        passed_ref[pl.ds(start, tile), :] = (outer * gate).astype(BF16)


def local_outputs(x_conv, maps_conv, z, step_rows, total_rows, skip, head_dim):
    length, channels = x_conv.shape
    width = 128
    columns = channels // width
    heads = channels // head_dim
    maps_width = maps_conv.shape[1]
    block = pl.BlockSpec((length, width), lambda i: (0, i))
    row_block = pl.BlockSpec((heads, length), lambda i: (0, 0))
    return pl.pallas_call(
        functools.partial(local_kernel, head_dim),
        grid=(columns,),
        in_specs=[
            block,
            pl.BlockSpec((length, maps_width), lambda i: (0, 0)),
            block,
            row_block,
            row_block,
            pl.BlockSpec(memory_space=pltpu.SMEM),
        ],
        out_specs=[block, block],
        out_shape=[jax.ShapeDtypeStruct((length, channels), BF16)] * 2,
        scratch_shapes=[pltpu.VMEM((length, length), F32)],
        compiler_params=params(),
        cost_estimate=pl.CostEstimate(
            flops=8_000_000_000, bytes_accessed=6_000_000, transcendentals=0
        ),
        name="local_outputs",
    )(x_conv, maps_conv, z, step_rows, total_rows, skip)


def fetches(sources, targets, columns, arrived):
    pieces = 4
    copies = []
    for index, (source, target) in enumerate(zip(sources, targets)):
        depth = target.shape[0] // pieces
        for piece in range(pieces):
            rows = pl.ds(piece * depth, depth)
            copies.append(
                pltpu.make_async_copy(
                    source.at[rows, columns],
                    target.at[rows, :],
                    arrived.at[index * pieces + piece],
                )
            )
    return copies


def norm_kernel(other, carried_ref, maps_ref, shown_ref, passed_ref, gain_ref, *rest):
    copies = []
    if other:
        out_ref, entering = rest
    else:
        sources, out_ref, targets, (entering, arrived) = rest[:2], rest[2], rest[3:5], rest[5:]
        copies = fetches(sources, targets, pl.ds(0, targets[0].shape[1]), arrived)
    for copy in copies:
        copy.start()
    state, channels = entering.shape
    pieces, depth, lanes = carried_ref.shape
    per_column = state // depth
    for piece in range(pieces):
        entering[
            pl.ds(depth * (piece % per_column), depth),
            pl.ds(lanes * (piece // per_column), lanes),
        ] = carried_ref[piece]
    ring = len(TURNS)
    size = out_ref.shape[0] // ring
    place = lax.axis_index("tp")
    across, core = place // 2, lax.rem(place, 2)
    if other:
        core = 1 - core
    for turn, ahead in enumerate(TURNS):
        pick = 2 * lax.rem(across + ahead, ring) + core
        rows = pl.ds(pl.multiple_of(pick * size, size), size)
        carry = jnp.dot(maps_ref[rows, state:], entering[...], preferred_element_type=F32)
        gated = shown_ref[rows, :].astype(F32) + carry * passed_ref[rows, :].astype(F32)
        scale = lax.rsqrt(jnp.mean(gated * gated, axis=1, keepdims=True) + 1e-05)
        out_ref[pl.ds(size * turn, size), :] = (gated * scale * gain_ref[...]).astype(BF16)
    for copy in copies:
        copy.wait()


def normed_rows(other, carried, maps_conv, shown, passed, gain, weights, name):
    length, channels = shown.shape
    state = maps_conv.shape[1] // 2
    near = pl.BlockSpec(memory_space=pltpu.VMEM)
    far = pl.BlockSpec(memory_space=pltpu.HBM)
    normed = jax.ShapeDtypeStruct((length // 2, channels), BF16)
    scratch = [pltpu.VMEM((state, channels), BF16)]
    fetched = []
    if not other:
        fetched = [jax.ShapeDtypeStruct((w.shape[0], w.shape[1] // 2), BF16) for w in weights]
        scratch.append(pltpu.SemaphoreType.DMA((8,)))
    return pl.pallas_call(
        functools.partial(norm_kernel, other),
        in_specs=[near] * 5 + [far] * len(weights),
        out_specs=[near] * (1 + len(fetched)),
        scratch_shapes=scratch,
        out_shape=[normed] + fetched,
        compiler_params=params(),
        cost_estimate=pl.CostEstimate(
            flops=1_000_000_000, bytes_accessed=3_000_000, transcendentals=0
        ),
        name=name,
    )(carried, maps_conv, shown, passed, gain, *[far_memory(weight) for weight in weights])


def project_near_kernel(own_ref, other_ref, own_weight_ref, other_weight_ref, *out_refs):
    rows, columns = out_refs[0].shape
    width = 512
    for start in range(0, columns, width):
        lanes = pl.ds(start, width)
        product = jnp.dot(own_ref[...], own_weight_ref[:, lanes], preferred_element_type=F32)
        product = product + jnp.dot(
            other_ref[...], other_weight_ref[:, lanes], preferred_element_type=F32
        )
        for index, out_ref in enumerate(out_refs):
            piece = product[rows * index : rows * (index + 1)]
            out_ref[:, lanes] = piece.astype(out_ref.dtype)


def project_far_kernel(own_ref, other_ref, own_weight_ref, other_weight_ref, *rest):
    out_refs, (own_near, other_near, arrived) = rest[:4], rest[4:]
    rows, columns = out_refs[0].shape
    width = 512
    first = own_weight_ref.shape[1] - columns
    copies = []
    for tile in range(columns // width):
        for index, (source, target) in enumerate(
            ((own_weight_ref, own_near), (other_weight_ref, other_near))
        ):
            copies.append(
                pltpu.make_async_copy(
                    source.at[:, pl.ds(first + tile * width, width)],
                    target.at[:, pl.ds(tile * width, width)],
                    arrived.at[2 * tile + index],
                )
            )
    for copy in copies:
        copy.start()
    for tile in range(columns // width):
        lanes = pl.ds(tile * width, width)
        copies[2 * tile].wait()
        copies[2 * tile + 1].wait()
        product = jnp.dot(own_ref[...], own_near[:, lanes], preferred_element_type=F32)
        product = product + jnp.dot(
            other_ref[...], other_near[:, lanes], preferred_element_type=F32
        )
        for index, out_ref in enumerate(out_refs):
            piece = product[rows * index : rows * (index + 1)]
            out_ref[:, lanes] = piece.astype(out_ref.dtype)


def project(own, other, own_weight, other_weight, columns, name):
    count, depth = own.shape
    near = pl.BlockSpec(memory_space=pltpu.VMEM)
    far = own_weight.shape[1] > columns
    weight_spec = pl.BlockSpec(memory_space=pltpu.HBM) if far else near
    weights = [own_weight, other_weight]
    return pl.pallas_call(
        project_far_kernel if far else project_near_kernel,
        in_specs=[near, near, weight_spec, weight_spec],
        out_specs=[near] * 4,
        out_shape=[jax.ShapeDtypeStruct((count // 4, columns), BF16)] * 4,
        scratch_shapes=[
            pltpu.VMEM((depth, columns), BF16),
            pltpu.VMEM((depth, columns), BF16),
            pltpu.SemaphoreType.DMA((8,)),
        ]
        if far
        else [],
        compiler_params=params(),
        cost_estimate=pl.CostEstimate(
            flops=4 * count * depth * columns, bytes_accessed=9_000_000, transcendentals=0
        ),
        name=name,
    )(own, other, *([far_memory(weight) for weight in weights] if far else weights))


def last_rows_kernel(x_ref, maps_ref, out_ref):
    count = out_ref.shape[0]
    channels = x_ref.shape[1]
    first = x_ref.shape[0] - count
    out_ref[:, :channels] = x_ref[...].astype(F32)[first:].astype(BF16)
    out_ref[:, channels:] = maps_ref[...].astype(F32)[first:].astype(BF16)


def last_rows(x, maps, count, held):
    last = x.shape[0] // held - 1
    tail = lambda array: pl.BlockSpec((held, array.shape[1]), lambda i: (last, 0))
    shape = (count, x.shape[1] + maps.shape[1])
    return pl.pallas_call(
        last_rows_kernel,
        grid=(1,),
        in_specs=[tail(x), tail(maps)],
        out_specs=pl.BlockSpec(memory_space=pltpu.VMEM),
        out_shape=jax.ShapeDtypeStruct(shape, BF16),
        compiler_params=params(),
        name="last_rows",
    )(x, maps)


def on_device(
    x_inputs,
    state_maps,
    z_gate,
    step_raw,
    step_bias,
    decay_log,
    skip_gain,
    x_filter,
    state_filter,
    norm_gain,
    out_weight,
):
    length, channels = x_inputs.shape
    leading = x_filter.shape[0] - 1
    heads = step_raw.shape[1]
    head_dim = channels // heads
    blocks = lax.axis_size("ctx")
    members = lax.axis_size("tp")
    ring = members // 2

    def core_swap(value):
        return lax.ppermute(value, "tp", [(i, i ^ 1) for i in range(members)])

    def along(value, steps):
        pairs = [
            (2 * y + c, 2 * ((y + steps) % ring) + c) for y in range(ring) for c in range(2)
        ]
        return lax.ppermute(value, "tp", pairs)

    held = 16
    x_inputs, state_maps = far_memory(x_inputs), far_memory(state_maps)
    halo = shifted(last_rows(x_inputs, state_maps, leading, held), "ctx", 1)
    x_filter, state_filter = far_memory(x_filter), far_memory(state_filter)
    conv, maps_conv, step, total, first_tail, reached = local_states(
        x_inputs,
        x_filter,
        state_maps,
        state_filter,
        far_memory(step_raw.T),
        far_memory(step_bias[None]),
        far_memory(decay_log[None]),
        blocks,
        held,
    )
    other_weight = core_swap(lax.optimization_barrier((out_weight, halo, first_tail))[0])
    x_conv, maps_conv, sent = first_rows(
        x_inputs,
        state_maps,
        halo,
        x_filter,
        state_filter,
        first_tail,
        reached,
        conv,
        maps_conv,
        held,
    )
    got = lax.all_to_all(sent, "ctx", 0, 0, tiled=True)
    shown, passed = local_outputs(
        x_conv,
        maps_conv,
        far_memory(z_gate),
        step,
        total,
        skip_gain,
        head_dim,
    )
    got, shown, passed = lax.optimization_barrier((got, shown, passed))
    entering = scan_blocks(got)
    carried = lax.all_to_all(entering, "ctx", 0, 0, tiled=True)

    gain = norm_gain[None]
    weights = (out_weight, other_weight)
    (give,) = normed_rows(True, carried, maps_conv, shown, passed, gain, (), "give_rows")
    taken = core_swap(give)
    keep, own_left, other_left = normed_rows(
        False, carried, maps_conv, shown, passed, gain, weights, "keep_rows"
    )
    columns = own_left.shape[1]
    far_a, up_a, down_a, own_a = project(keep, taken, own_left, other_left, columns, "left_half")
    far_b, up_b, down_b, own_b = project(
        keep, taken, out_weight, other_weight, columns, "right_half"
    )

    def added(*values):
        return functools.reduce(lambda a, b: a + b, [v.astype(F32) for v in values]).astype(BF16)

    relay_a = along(far_a, 1)
    from_above_a = along(down_a, -1)
    relay_b = along(far_b, -1)
    from_below_b = along(up_b, 1)
    from_below_a = along(added(up_a, relay_a), 1)
    from_above_b = along(added(down_b, relay_b), -1)
    return jnp.concatenate(
        [added(own_a, from_above_a, from_below_a), added(own_b, from_above_b, from_below_b)], axis=1
    )


def solution(mesh):
    return jax.shard_map(
        on_device,
        mesh=mesh,
        in_specs=(
            P("ctx", "tp"),
            P("ctx", "tp"),
            P("ctx", "tp"),
            P("ctx", "tp"),
            P("tp"),
            P("tp"),
            P("tp"),
            P(None, "tp"),
            P(None, "tp"),
            P("tp"),
            P("tp", None),
        ),
        out_specs=P(("ctx", "tp"), None),
        check_vma=False,
    )
```
